128 devices in a mesh: row: 8 (over z, core), col: 16 (over y, x).
Axes of the slice: x: 4, y: 4, z: 4, core: 2. Of those that a mesh axis runs over, the one named last changes fastest.
Arguments:
- tokens: bfloat16 [512, 8192], P('row', 'col'), may hold values from -6 to 6
- weights: bfloat16 [2, 8192, 28672], P(None, 'col', 'row'), may hold values from -2 to 2
- adapter_in: bfloat16 [2, 64, 8192], P(None, None, 'col'), may hold values from -0.75 to 0.75
- adapter_out: bfloat16 [2, 64, 28672], P(None, None, 'row'), may hold values from -0.3 to 0.3
- magnitude: float32 [2, 28672], P(None, 'row'), may hold values from 0.5 to 2
- hidden_cot: bfloat16 [512, 28672], P('col', 'row'), may hold values from -0.29882812 to 0.29882812
Outputs:
- hidden: bfloat16 [512, 28672], P('col', 'row')
- grad_in: float32 [2, 64, 8192], P(None, None, 'col')
- grad_out: float32 [2, 64, 28672], P(None, None, 'row')
- grad_mag: float32 [2, 28672], P(None, 'row')
The draws below stay inside these ranges and needn't reach their ends.
All inputs are finite; a program needn't handle non-finite values.
Results may differ from the reference program's by a relative error of at most 0.028.
Values may be sent and summed in bfloat16 or wider, within the bound.
A program may use at most 192 MiB of HBM per device.

```python
import math
import jax
import jax.numpy as jnp
from jax import lax

D = 8192
FF = 28672
R = 64
TOKENS = 512
N_COL = 16


def factor_draws(key):
    key_left, key_right, key_extra = jax.random.split(jax.random.fold_in(key, 29), 3)
    left = jax.random.truncated_normal(key_left, -6.0, 6.0, (2, R, D), jnp.float32)
    right = jax.random.truncated_normal(key_right, -6.0, 6.0, (2, R, FF), jnp.float32)
    extra = jax.random.truncated_normal(key_extra, -6.0, 6.0, (2, R, FF), jnp.float32)
    left_bf = (0.125 * left).astype(jnp.bfloat16)
    right_bf = (0.05 * right).astype(jnp.bfloat16)
    return (left_bf, right_bf, 0.05 * extra)


def draw_adapter_in(key, part):
    return factor_draws(key)[0]


def draw_adapter_out(key, part):
    return factor_draws(key)[1]


def draw_weights(key, part):
    left_bf, right_bf, extra = factor_draws(key)
    key_base, key_rows, key_cols = jax.random.split(jax.random.fold_in(key, 11), 3)
    base = jax.random.truncated_normal(key_base, -4.0, 4.0, (2, D, FF), jnp.float32)
    row_scale = 10.0 ** jax.random.uniform(key_rows, (2, D, 1), jnp.float32)
    col_scale = 10.0 ** jax.random.uniform(key_cols, (2, 1, FF), jnp.float32)
    trend = 3.0 ** (0.5 * jnp.arange(D, dtype=jnp.float32) / D)
    values = base * row_scale * col_scale * trend[None, :, None] / (5.0 * D ** 0.5)
    earlier = extra - 0.8 * right_bf.astype(jnp.float32)
    planted = jnp.einsum('prd,prf->pdf', left_bf.astype(jnp.float32), earlier, precision=lax.Precision.HIGHEST)
    values = jnp.clip(values + planted, -2.0, 2.0)
    return values.astype(jnp.bfloat16)


def shard_levels(stream_key, shape, cuts, least, top_value):
    level, own = 1.0, jax.random.fold_in(stream_key, 6)
    for axis_at, parts in cuts:
        heights = jnp.exp(jax.random.uniform(jax.random.fold_in(own, axis_at), (parts,), jnp.float32, least / len(cuts), top_value / len(cuts)))
        level = level * jnp.repeat(heights, shape[axis_at] // parts).reshape([-1 if axis == axis_at else 1 for axis in range(len(shape))])
    return level


def centred(rng, extent, width, reach, cuts=(), held_as=jnp.bfloat16):
    values = width * jax.random.normal(rng, extent, jnp.float32)
    if cuts:
        values = values * shard_levels(rng, extent, cuts, -0.22, 0.18)
    return jnp.clip(values, -reach, reach).astype(held_as)


def setup_inputs(seed: int = 0) -> dict:
    key_list = jax.random.split(jax.random.key(seed), 7)
    tokens = centred(key_list[0], (TOKENS, D), 1.0, 6.0, ((0, 8), (1, 16)))
    weights = draw_weights(jax.random.fold_in(key_list[6], 71), 0)
    adapter_in = draw_adapter_in(jax.random.fold_in(key_list[6], 71), 0)
    adapter_out = draw_adapter_out(jax.random.fold_in(key_list[6], 71), 0)
    magnitude = jnp.clip(jnp.exp(math.log(2.0) - 1.3862944 * jax.random.uniform(key_list[4], (2, FF), jnp.float32) ** shard_levels(key_list[4], (2, FF), ((1, 8),), -0.2, 0.2)), 0.5, 2.0)
    hidden_cot = centred(key_list[5], (TOKENS, FF), 0.05, 0.29882812, ((0, 16), (1, 8)))
    return dict(tokens=tokens, weights=weights, adapter_in=adapter_in, adapter_out=adapter_out, magnitude=magnitude, hidden_cot=hidden_cot)


EPSILON = 1e-06

def project(tokens, merged):
    width_block = D // N_COL
    blocks_x = tokens.reshape(TOKENS, N_COL, width_block).transpose(1, 0, 2)
    blocks_w = merged.reshape(N_COL, width_block, FF)

    def add_block(running, pair):
        product = jnp.dot(pair[0], pair[1], preferred_element_type=jnp.float32).astype(jnp.bfloat16)
        product = lax.optimization_barrier(product)
        return (running + product.astype(jnp.float32), None)
    running, _ = lax.scan(add_block, jnp.zeros((TOKENS, FF), jnp.float32), (blocks_x, blocks_w))
    return running

def reference(tokens, weights, adapter_in, adapter_out, magnitude, hidden_cot):
    directions = []
    norms = []
    pres = []
    for index in range(2):
        low_rank = jnp.dot(adapter_in[index].T, adapter_out[index], preferred_element_type=jnp.float32)
        direction = weights[index].astype(jnp.float32) + low_rank
        column_norm = jnp.sqrt(lax.optimization_barrier(jnp.sum(direction * direction, axis=0)) + EPSILON)
        merged = (direction * (magnitude[index] / column_norm)[None, :]).astype(jnp.bfloat16)
        pres.append(project(tokens, merged))
        directions.append(direction)
        norms.append(column_norm)
    gate, up_proj = (pres[0], pres[1])
    sigmoid_g = jax.nn.sigmoid(gate)
    hidden = (gate * sigmoid_g * up_proj).astype(jnp.bfloat16)
    cot_float = hidden_cot.astype(jnp.float32)
    d_pre = [(cot_float * up_proj * sigmoid_g * (1.0 + gate * (1.0 - sigmoid_g))).astype(jnp.bfloat16), (cot_float * gate * sigmoid_g).astype(jnp.bfloat16)]
    grads_in = []
    grads_out = []
    grads_mag = []
    for index in range(2):
        grad_weight = jnp.dot(tokens.T, d_pre[index], preferred_element_type=jnp.float32)
        direction = directions[index]
        column_norm = norms[index]
        statistic = lax.optimization_barrier(jnp.sum(grad_weight * direction, axis=0))
        grads_mag.append(statistic / column_norm)
        coef_grad = magnitude[index] / column_norm
        coef_dir = magnitude[index] * statistic / column_norm ** 3
        d_direction = coef_grad[None, :] * grad_weight - coef_dir[None, :] * direction
        grads_in.append(jnp.dot(adapter_out[index].astype(jnp.float32), d_direction.T, precision=lax.Precision.HIGHEST))
        grads_out.append(jnp.dot(adapter_in[index].astype(jnp.float32), d_direction, precision=lax.Precision.HIGHEST))
    return (hidden, jnp.stack(grads_in), jnp.stack(grads_out), jnp.stack(grads_mag))
```

```python
import jax
import jax.numpy as jnp
from jax import lax
from jax.sharding import PartitionSpec as P

EPSILON = 1e-06
F32 = jnp.float32
BF16 = jnp.bfloat16


def on_device(tokens, weights, adapter_in, adapter_out, magnitude, hidden_cot):
    token_all = lax.all_gather(tokens, "row", axis=0, tiled=True)
    low_rank = jnp.einsum("prd,prf->pdf", adapter_in, adapter_out, preferred_element_type=F32)
    direction = weights.astype(F32) + low_rank
    square_sum = lax.psum(jnp.sum(direction * direction, axis=1), "col")
    direction_b = direction.astype(BF16)
    partial_value = jnp.einsum("td,pdf->ptf", token_all, direction_b, preferred_element_type=F32)
    raw = lax.psum_scatter(
        partial_value.astype(BF16), "col", scatter_dimension=1, tiled=True
    ).astype(F32)
    rank_tok = jnp.einsum("prd,td->prt", adapter_in, token_all, preferred_element_type=F32)
    rank_own = lax.psum_scatter(rank_tok, "col", scatter_dimension=2, tiled=True)
    column_norm = jnp.sqrt(square_sum + EPSILON)
    coef = magnitude / column_norm
    gate = raw[0] * coef[0]
    up = raw[1] * coef[1]
    sig = jax.nn.sigmoid(gate)
    hidden = (gate * sig * up).astype(BF16)
    cot = hidden_cot.astype(F32)
    d_gate = (cot * up * sig * (1.0 + gate * (1.0 - sig))).astype(BF16)
    d_up = (cot * gate * sig).astype(BF16)
    d_pre = jnp.stack((d_gate, d_up), axis=0)
    statistic = lax.psum(jnp.sum(d_pre.astype(F32) * raw, axis=1), "col")
    grad_mag = statistic / column_norm
    coef_dir = magnitude * statistic / column_norm**3
    first = jnp.einsum("prt,ptf->prf", rank_own.astype(BF16), d_pre, preferred_element_type=F32)
    second = jnp.einsum("prd,pdf->prf", adapter_in, direction_b, preferred_element_type=F32)
    grad_out = lax.psum(
        (coef[:, None, :] * first - coef_dir[:, None, :] * second).astype(BF16), "col"
    ).astype(F32)
    out_f = adapter_out.astype(F32)
    scaled = (out_f * coef[:, None, :]).astype(BF16)
    row_tok = jnp.einsum("prf,ptf->prt", scaled, d_pre, preferred_element_type=F32)
    row_all = lax.all_gather(row_tok.astype(BF16), "col", axis=2, tiled=True)
    left = jnp.einsum("prt,td->prd", row_all, token_all, preferred_element_type=F32)
    tilted = (out_f * coef_dir[:, None, :]).astype(BF16)
    left = left - jnp.einsum("prf,pdf->prd", tilted, direction_b, preferred_element_type=F32)
    grad_in = lax.psum(left.astype(BF16), "row").astype(F32)
    return (hidden, grad_in, grad_out, grad_mag)


def solution(mesh):
    in_specs = (
        P("row", "col"),
        P(None, "col", "row"),
        P(None, None, "col"),
        P(None, None, "row"),
        P(None, "row"),
        P("col", "row"),
    )
    out_specs = (P("col", "row"), P(None, None, "col"), P(None, None, "row"), P(None, "row"))
    return jax.shard_map(
        on_device, mesh=mesh, in_specs=in_specs, out_specs=out_specs, check_vma=False
    )
```

```python
import functools

import jax
import jax.numpy as jnp
from jax import lax
from jax.experimental import pallas as pl
from jax.experimental.pallas import tpu as pltpu
from jax.sharding import PartitionSpec as P

EPSILON = 1e-06
F32 = jnp.float32
BF16 = jnp.bfloat16
MESH = pl.DeviceIdType.MESH
SIDE = 4
ORDER = (2, 1, 3, 0)
EXCHANGES = 17
FAR, RAW, ACC = 0, 1, 2


def nt_dot(a, b):
    return lax.dot_general(a, b, (((1,), (1,)), ((), ())), preferred_element_type=F32)


def kernel(n_row, tok, w_hbm, ain, aout, mag, cot, hid, gi, go, gm,
           lhs, wb, pp, ain_t, rfar, rnear, sfar, snear, cotq, ssb, ssx, ssr, ssr2,
           zb, zx, zs, zr, zr2, hidq, hidr, dsc, st, strr, bb, ball, g1, g1r,
           wv, wx, wr, wall, gall0, gall1, gib, gir, gio, giall,
           w_sem, tok_s, tok_r, main_s, main_r, ph2_s, ph2_r, ex_s, ex_r):
    row, col = lax.axis_index("row"), lax.axis_index("col")
    y, x = col // SIDE, col % SIDE
    n_z = n_row // 2
    z, core = row // 2, row % 2
    share, depth = tok.shape
    rank = ain.shape[1]
    width = aout.shape[2]
    fq = width // SIDE
    tb = share * n_row // SIDE
    rq = rank // SIDE
    rb = tb + rq
    own_rows = tb // SIDE
    half = ((rb // 16 + 1) // 2) * 16
    top, bottom = pl.ds(0, half), pl.ds(half, rb - half)
    first, second = (x, y), (y, x)

    def wrap(v):
        return (v + 2 * SIDE) % SIDE

    def at_x(k):
        return (row, y * SIDE + wrap(x + k))

    def at_y(k):
        return (row, wrap(y + k) * SIDE + x)

    def at_row(k):
        return ((row + k) % n_row, col)

    def at_core():
        return (z * 2 + (1 - core), col)

    def at_z(k):
        return (((z + k) % n_z) * 2 + core, col)

    ring1 = (at_x, at_y)
    ring2 = (at_y, at_x)

    def w_copy(p, q):
        lanes = pl.ds(pl.multiple_of(q * fq, 128), fq)
        return pltpu.make_async_copy(w_hbm.at[p, :, lanes], wb.at[p, q], w_sem.at[p * SIDE + q])

    for j in ORDER:
        for p in range(2):
            w_copy(p, wrap(x + j)).start()

    barrier = pltpu.get_barrier_semaphore()
    peers = [at_x(k) for k in (1, 2, 3)] + [at_y(k) for k in (1, 2, 3)]
    peers += [at_row(k) for k in range(1, n_row)]
    for peer in peers:
        pl.semaphore_signal(barrier, inc=1, device_id=peer, device_id_type=MESH)
    pl.semaphore_wait(barrier, len(peers))

    def remote(src, dst, send, recv, peer):
        return pltpu.make_async_remote_copy(
            src_ref=src, dst_ref=dst, send_sem=send, recv_sem=recv,
            device_id=peer, device_id_type=MESH)

    def tok_rows(owner):
        start = owner * share
        offset = (start // tb) * rb + start % tb
        return lhs.at[0, pl.ds(pl.multiple_of(offset, 16), share), :]

    def tok_copy(i):
        if i == 0:
            src, dst, peer = tok, tok_rows(row), at_core()
        elif i < n_z:
            src, dst, peer = tok, tok_rows(row), at_z(i)
        else:
            owner = ((z + n_z - (i - n_z + 1)) % n_z) * 2 + core
            src, dst, peer = tok_rows(owner), tok_rows(owner), at_core()
        return remote(src, dst, tok_s.at[i], tok_r.at[i], peer)

    n_tok = 2 * n_z - 1
    for i in [1, n_z - 1] + list(range(2, n_z - 1)) + [0]:
        tok_copy(i).start()

    def exchange(e, peer_of, count, src, dst):
        return [remote(src(k), dst(k), ex_s.at[e * 8 + k], ex_r.at[e * 8 + k], peer_of(k))
                for k in range(1, count)]

    started = []

    def begin(copies):
        for c in copies:
            c.start()
        started.extend(copies)
        return copies

    def arrive(copies):
        for c in copies:
            c.wait_recv()

    def quarter(q):
        return pl.ds(pl.multiple_of(q * fq, 128), fq)

    cot_x = begin(exchange(0, at_x, SIDE, lambda k: cot.at[:, quarter(wrap(x + k))],
                           lambda k: cotq.at[x]))

    ssb[...] = jnp.zeros_like(ssb)
    for p in range(2):
        ain_t[p] = ain[p].astype(F32).T.astype(BF16)
        for b in range(SIDE):
            lhs[p, b * rb + tb:(b + 1) * rb, :] = ain[p, b * rq:(b + 1) * rq, :]
    own_off = ((row * share) // tb) * rb + (row * share) % tb
    lhs[0, pl.ds(pl.multiple_of(own_off, 16), share), :] = tok[...]
    cotq[x] = cot[:, quarter(x)]

    def direction(p, q):
        w_copy(p, q).wait()
        left = aout[p, :, quarter(q)]
        step = min(128, depth)

        def body(i, acc):
            rows = pl.ds(pl.multiple_of(i * step, step), step)
            low = jnp.dot(ain_t[p, rows, :], left, preferred_element_type=F32)
            d = wb[p, q, rows, :].astype(F32) + low
            wb[p, q, rows, :] = d.astype(BF16)
            return acc + jnp.sum((d * d).reshape(step // 8, 8, fq), axis=0)

        acc = lax.fori_loop(0, depth // step, body, jnp.zeros((8, fq), F32))
        ssb[q, p:p + 1, :] = jnp.sum(acc, axis=0, keepdims=True)

    def product(p, q):
        res = jnp.dot(lhs[p], wb[p, q], preferred_element_type=F32).astype(BF16)
        for b in range(SIDE):
            piece = res[b * rb:(b + 1) * rb, :]
            if p == 0:
                pp[0, q, b] = piece
            else:
                pp[1, b, q] = piece

    def main_copy(p, d, kind, j):
        c1, s = first[p], wrap(second[p] + j)
        peer = ring1[p](1 if d == 0 else -1)
        if kind == FAR:
            rows = top if d == 0 else bottom
            src = pp.at[p, wrap(c1 + 2), s, rows, :]
            dst = rfar.at[p, j, rows, :]
        else:
            rows = top if (d == 0) == (kind == ACC) else bottom
            src = pp.at[p, wrap(c1 + (1 if d == 0 else -1)), s, rows, :]
            dst = rnear.at[p, d, j, rows, :]
        i = ((p * 2 + d) * 3 + kind) * SIDE + j
        return remote(src, dst, main_s.at[i], main_r.at[i], peer)

    def ph2_copy(p, d, kind):
        c1, c2 = first[p], second[p]
        peer = ring2[p](1 if d == 0 else -1)
        if kind == FAR:
            rows = top if d == 0 else bottom
            src = pp.at[p, c1, wrap(c2 + 2), rows, :]
            dst = sfar.at[p, rows, :]
        else:
            rows = top if (d == 0) == (kind == ACC) else bottom
            src = pp.at[p, c1, wrap(c2 + (1 if d == 0 else -1)), rows, :]
            dst = snear.at[p, d, rows, :]
        i = (p * 2 + d) * 3 + kind
        return remote(src, dst, ph2_s.at[i], ph2_r.at[i], peer)

    def stage(m, carry):
        j_dir = (2 - m + 3 * ((m * (m - 1)) // 2) + 8) % SIDE
        i_p = m - 2
        j_p = (2 - i_p + 3 * ((i_p * (i_p - 1)) // 2) + 8) % SIDE

        @pl.when(m == 2)
        def _():
            for i in [1, n_z - 1] + list(range(2, n_z - 1)):
                tok_copy(i).wait_recv()
                tok_copy(n_z - 1 + i).start()
            tok_copy(0).wait_recv()
            for i in range(n_z, n_tok):
                tok_copy(i).wait_recv()
            for b in range(SIDE):
                lhs[1, b * rb:b * rb + tb, :] = lhs[0, b * rb:b * rb + tb, :]

        @pl.when(m >= 2)
        def _():
            q = wrap(x + j_p)
            product(0, q)

            @pl.when(i_p == 0)
            def _():
                for j in ORDER:
                    for d in range(2):
                        main_copy(0, d, FAR, j).start()

            @pl.when(i_p == 1)
            def _():
                for j in ORDER:
                    main_copy(0, 0, RAW, j).start()

            @pl.when(i_p == 2)
            def _():
                for j in ORDER:
                    main_copy(0, 1, RAW, j).start()

            product(1, q)
            for d in range(2):
                main_copy(1, d, FAR, j_p).start()
            for d in range(2):
                main_copy(1, d, RAW, j_p).start()

        @pl.when(m < SIDE)
        def _():
            q = wrap(x + j_dir)
            for p in range(2):
                direction(p, q)

        return carry

    lax.fori_loop(0, SIDE + 2, stage, 0)

    ss_x = begin(exchange(1, at_x, SIDE, lambda k: ssb.at[wrap(x + k)], lambda k: ssr.at[k]))
    ain_all = ain[...].reshape(2 * rank, depth)
    for b in range(SIDE):
        zb[b] = nt_dot(ain_all, lhs[0, b * rb:b * rb + tb, :]).astype(BF16)
    z_y = begin(exchange(3, at_y, SIDE, lambda k: zb.at[wrap(y + k)], lambda k: zr.at[k]))

    def add_into(dst, src):
        dst[...] = (dst[...].astype(F32) + src[...].astype(F32)).astype(BF16)

    for j in ORDER:
        for p in range(2):
            for d in range(2):
                main_copy(p, d, FAR, j).wait_recv()
                rows = top if d == 0 else bottom
                near = wrap(first[p] + (1 if d == 0 else -1))
                add_into(pp.at[p, near, wrap(second[p] + j), rows, :], rfar.at[p, j, rows, :])
                main_copy(p, d, ACC, j).start()

    arrive(ss_x)
    ssx[...] = ssb[x] + ssr[1] + ssr[2] + ssr[3]
    ss_y = begin(exchange(2, at_y, SIDE, lambda k: ssx, lambda k: ssr2.at[k]))
    arrive(z_y)
    zx[...] = (zb[y].astype(F32) + zr[1].astype(F32) + zr[2].astype(F32)
               + zr[3].astype(F32)).astype(BF16)
    z_x = begin(exchange(4, at_x, SIDE, lambda k: zx, lambda k: zr2.at[k]))

    for j in ORDER:
        for p in range(2):
            for d in range(2):
                main_copy(p, d, RAW, j).wait_recv()
                main_copy(p, d, ACC, j).wait_recv()
            mine = pp.at[p, first[p], wrap(second[p] + j)]
            mine[...] = (mine[...].astype(F32) + rnear[p, 0, j].astype(F32)
                         + rnear[p, 1, j].astype(F32)).astype(BF16)
            if j == 2:
                for d in range(2):
                    ph2_copy(p, d, FAR).start()
            elif j == 1:
                ph2_copy(p, 0, RAW).start()
            elif j == 3:
                ph2_copy(p, 1, RAW).start()

    arrive(ss_y)
    total = ssx[0:2] + ssr2[1, 0:2] + ssr2[2, 0:2] + ssr2[3, 0:2]
    norm = jnp.sqrt(total + EPSILON)
    mag_q = mag[:, quarter(x)]
    coef = mag_q / norm
    arrive(z_x)
    zs[...] = (zx[...].astype(F32) + zr2[1].astype(F32) + zr2[2].astype(F32)
               + zr2[3].astype(F32)).astype(BF16)
    arrive(cot_x)

    for p in range(2):
        for d in range(2):
            ph2_copy(p, d, FAR).wait_recv()
            rows = top if d == 0 else bottom
            near = wrap(second[p] + (1 if d == 0 else -1))
            add_into(pp.at[p, first[p], near, rows, :], sfar.at[p, rows, :])
            ph2_copy(p, d, ACC).start()
    for p in range(2):
        for d in range(2):
            ph2_copy(p, d, RAW).wait_recv()
            ph2_copy(p, d, ACC).wait_recv()

    def summed(p, rows):
        return (pp[p, first[p], second[p], rows, :].astype(F32)
                + snear[p, 0, rows, :].astype(F32) + snear[p, 1, rows, :].astype(F32))

    coef0, coef1 = coef[0:1], coef[1:2]
    chunk = min(16, own_rows)
    per = own_rows // chunk

    def gating(i, carry):
        acc0, acc1 = carry
        rows = pl.ds(pl.multiple_of(i * chunk, chunk), chunk)
        inner = pl.ds(pl.multiple_of((i % per) * chunk, chunk), chunk)
        raw0, raw1 = summed(0, rows), summed(1, rows)
        gate, up = raw0 * coef0, raw1 * coef1
        sig = jax.nn.sigmoid(gate)
        hidq[i // per, inner, :] = (gate * sig * up).astype(BF16)
        c = cotq[i // per, inner, :].astype(F32)
        d0 = (c * up * sig * (1.0 + gate * (1.0 - sig))).astype(BF16)
        d1 = (c * gate * sig).astype(BF16)
        dsc[0, rows, :] = d0
        dsc[1, rows, :] = d1
        s0 = jnp.sum((d0.astype(F32) * raw0).reshape(chunk // 8, 8, fq), axis=0)
        s1 = jnp.sum((d1.astype(F32) * raw1).reshape(chunk // 8, 8, fq), axis=0)
        return (acc0 + s0, acc1 + s1)

    zero = jnp.zeros((8, fq), F32)
    acc0, acc1 = lax.fori_loop(0, tb // chunk, gating, (zero, zero))
    st[...] = zero
    st[0:1] = jnp.sum(acc0, axis=0, keepdims=True)
    st[1:2] = jnp.sum(acc1, axis=0, keepdims=True)
    st_y = begin(exchange(6, at_y, SIDE, lambda k: st, lambda k: strr.at[k]))

    for p in range(2):
        res = jnp.dot(zs[p * rank:(p + 1) * rank, :], dsc[p], preferred_element_type=F32)
        for b in range(SIDE):
            g1[b, p] = res[b * rq:(b + 1) * rq, :].astype(BF16)
    g1_y = begin(exchange(8, at_y, SIDE, lambda k: g1.at[wrap(y + k)], lambda k: g1r.at[k]))
    for p in range(2):
        scaled = (aout[p, :, quarter(x)].astype(F32) * coef[p:p + 1]).astype(BF16)
        wv[p * rank:(p + 1) * rank, :] = nt_dot(scaled, dsc[p]).astype(BF16)
    w_x = begin(exchange(9, at_x, SIDE, lambda k: wv, lambda k: wr.at[k]))
    hid_x = begin(exchange(5, at_x, SIDE, lambda k: hidq.at[wrap(x + k)], lambda k: hidr.at[x]))
    hidr[x] = hidq[x]

    arrive(st_y)
    stat = st[0:2] + strr[1, 0:2] + strr[2, 0:2] + strr[3, 0:2]
    tilt = mag_q * stat / (norm * norm * norm)
    bb[...] = zero
    bb[0:2] = tilt
    bb[2:4] = stat / norm
    b_x = begin(exchange(7, at_x, SIDE, lambda k: bb, lambda k: ball.at[x]))
    ball[x] = bb[...]

    arrive(g1_y)
    for p in range(2):
        both = (g1[y, p].astype(F32) + g1r[1, p].astype(F32) + g1r[2, p].astype(F32)
                + g1r[3, p].astype(F32))
        piece = coef[p:p + 1] * both - tilt[p:p + 1] * summed(p, pl.ds(tb, rq))
        if p == 0:
            gall0[y, x] = piece.astype(BF16)
        else:
            gall1[x, y] = piece.astype(BF16)
    ga_x = begin(exchange(11, at_x, SIDE, lambda k: gall0.at[y, x], lambda k: gall0.at[y, x]))
    gb_y = begin(exchange(13, at_y, SIDE, lambda k: gall1.at[x, y], lambda k: gall1.at[x, y]))

    arrive(w_x)
    wx[...] = (wv[...].astype(F32) + wr[1].astype(F32) + wr[2].astype(F32)
               + wr[3].astype(F32)).astype(BF16)
    w_y = begin(exchange(10, at_y, SIDE, lambda k: wx, lambda k: wall.at[y]))
    wall[y] = wx[...]

    arrive(ga_x)
    ga_y = begin(exchange(12, at_y, SIDE, lambda k: gall0.at[y], lambda k: gall0.at[y]))
    arrive(gb_y)
    gb_x = begin(exchange(14, at_x, SIDE, lambda k: gall1.at[x], lambda k: gall1.at[x]))

    arrive(b_x)
    arrive(w_y)
    out_rows = 2 * rank // n_row
    for p in range(2):
        total_in = jnp.zeros((rank, depth), F32)
        for b in range(SIDE):
            total_in = total_in + jnp.dot(
                wall[b, p * rank:(p + 1) * rank, :], lhs[0, b * rb:b * rb + tb, :],
                preferred_element_type=F32)
        for q in range(SIDE):
            scaled = (aout[p, :, q * fq:(q + 1) * fq].astype(F32) * ball[q, p:p + 1]).astype(BF16)
            total_in = total_in - nt_dot(scaled, wb[p, q])
        for b in range(rank // out_rows):
            gib[p * (rank // out_rows) + b] = total_in[b * out_rows:(b + 1) * out_rows].astype(BF16)
    gi_rs = begin(exchange(15, at_row, n_row, lambda k: gib.at[(row + k) % n_row],
                           lambda k: gir.at[k]))

    for q in range(SIDE):
        gm[:, q * fq:(q + 1) * fq] = ball[q, 2:4, :]
    arrive(hid_x)
    for q in range(SIDE):
        hid[:, q * fq:(q + 1) * fq] = hidr[q]

    arrive(gi_rs)
    acc = gib[row].astype(F32)
    for k in range(1, n_row):
        acc = acc + gir[k].astype(F32)
    gio[...] = acc.astype(BF16)
    gi_ag = begin(exchange(16, at_row, n_row, lambda k: gio, lambda k: giall.at[row]))
    giall[row] = gio[...]

    arrive(ga_y)
    arrive(gb_x)
    for q in range(SIDE):
        for b in range(SIDE):
            go[0, b * rq:(b + 1) * rq, q * fq:(q + 1) * fq] = gall0[b, q]
            go[1, b * rq:(b + 1) * rq, q * fq:(q + 1) * fq] = gall1[q, b]
    arrive(gi_ag)
    for p in range(2):
        for b in range(rank // out_rows):
            gi[p, b * out_rows:(b + 1) * out_rows, :] = giall[p * (rank // out_rows) + b]

    for i in range(n_tok):
        tok_copy(i).wait_send()
    for p in range(2):
        for d in range(2):
            for kind in range(3):
                for j in range(SIDE):
                    main_copy(p, d, kind, j).wait_send()
                ph2_copy(p, d, kind).wait_send()
    for c in started:
        c.wait_send()


def solution(mesh):
    n_row = mesh.shape["row"]

    def on_device(tokens, weights, adapter_in, adapter_out, magnitude, hidden_cot):
        share, depth = tokens.shape
        rank = adapter_in.shape[1]
        width = adapter_out.shape[2]
        fq = width // SIDE
        tb = share * n_row // SIDE
        rq = rank // SIDE
        rb = tb + rq
        own_rows = tb // SIDE
        pr = 2 * rank
        vm = pltpu.VMEM
        dma = pltpu.SemaphoreType.DMA
        scratch = [
            vm((2, SIDE * rb, depth), BF16),
            vm((2, SIDE, depth, fq), BF16),
            vm((2, SIDE, SIDE, rb, fq), BF16),
            vm((2, depth, rank), BF16),
            vm((2, SIDE, rb, fq), BF16),
            vm((2, 2, SIDE, rb, fq), BF16),
            vm((2, rb, fq), BF16),
            vm((2, 2, rb, fq), BF16),
            vm((SIDE, own_rows, fq), BF16),
            vm((SIDE, 8, fq), F32),
            vm((8, fq), F32),
            vm((SIDE, 8, fq), F32),
            vm((SIDE, 8, fq), F32),
            vm((SIDE, pr, tb), BF16),
            vm((pr, tb), BF16),
            vm((pr, tb), BF16),
            vm((SIDE, pr, tb), BF16),
            vm((SIDE, pr, tb), BF16),
            vm((SIDE, own_rows, fq), BF16),
            vm((SIDE, own_rows, fq), BF16),
            vm((2, tb, fq), BF16),
            vm((8, fq), F32),
            vm((SIDE, 8, fq), F32),
            vm((8, fq), F32),
            vm((SIDE, 8, fq), F32),
            vm((SIDE, 2, rq, fq), BF16),
            vm((SIDE, 2, rq, fq), BF16),
            vm((pr, tb), BF16),
            vm((pr, tb), BF16),
            vm((SIDE, pr, tb), BF16),
            vm((SIDE, pr, tb), BF16),
            vm((SIDE, SIDE, rq, fq), BF16),
            vm((SIDE, SIDE, rq, fq), BF16),
            vm((n_row, pr // n_row, depth), BF16),
            vm((n_row, pr // n_row, depth), BF16),
            vm((pr // n_row, depth), BF16),
            vm((n_row, pr // n_row, depth), BF16),
            dma((2 * SIDE,)),
            dma((n_row,)),
            dma((n_row,)),
            dma((12 * SIDE,)),
            dma((12 * SIDE,)),
            dma((12,)),
            dma((12,)),
            dma((EXCHANGES * 8,)),
            dma((EXCHANGES * 8,)),
        ]
        vmem = pl.BlockSpec(memory_space=pltpu.VMEM)
        hidden, grad_in, grad_out, grad_mag = pl.pallas_call(
            functools.partial(kernel, n_row),
            out_shape=(
                jax.ShapeDtypeStruct(hidden_cot.shape, BF16),
                jax.ShapeDtypeStruct(adapter_in.shape, BF16),
                jax.ShapeDtypeStruct(adapter_out.shape, BF16),
                jax.ShapeDtypeStruct(magnitude.shape, F32),
            ),
            in_specs=[vmem, pl.BlockSpec(memory_space=pl.ANY), vmem, vmem, vmem, vmem],
            out_specs=(vmem, vmem, vmem, vmem),
            scratch_shapes=scratch,
            compiler_params=pltpu.CompilerParams(
                collective_id=0, has_side_effects=True, vmem_limit_bytes=60 * 2**20
            ),
        )(tokens, weights, adapter_in, adapter_out, magnitude, hidden_cot)
        return (hidden, grad_in.astype(F32), grad_out.astype(F32), grad_mag)

    in_specs = (
        P("row", "col"),
        P(None, "col", "row"),
        P(None, None, "col"),
        P(None, None, "row"),
        P(None, "row"),
        P("col", "row"),
    )
    out_specs = (P("col", "row"), P(None, None, "col"), P(None, None, "row"), P(None, "row"))
    return jax.shard_map(
        on_device, mesh=mesh, in_specs=in_specs, out_specs=out_specs, check_vma=False
    )
```

```python
import functools

import jax
import jax.numpy as jnp
from jax import lax
from jax.experimental import pallas as pl
from jax.experimental.pallas import tpu as pltpu
from jax.sharding import PartitionSpec as P

EPSILON = 1e-06
F32 = jnp.float32
BF16 = jnp.bfloat16
MESH = pl.DeviceIdType.MESH
SIDE = 4
ORDER = (2, 1, 3, 0)
EXCHANGES = 19
FAR, RAW, ACC = 0, 1, 2


def nt_dot(a, b):
    return lax.dot_general(a, b, (((1,), (1,)), ((), ())), preferred_element_type=F32)


def kernel(n_row, tok, w_hbm, ain, aout, mag, cot, hid_out, gi_out, go_out, gm_out,
           lhs, wb, pp, ainv, aoutv, magv, ain_t, rfar, rnear, sfar, snear, cotq, ssb, ssx, ssr, ssr2,
           zb, zx, zs, zr, zr2, hidq, hidr, dsc, st, strr, bb, ball, gmq, g1, g1r,
           wv, wx, wr, wall, qq, qr, qx, qr2, gall, gib, gir, gio, giall, tin,
           w_sem, in_sem, out_sem, tok_s, tok_r, main_s, main_r, ph2_s, ph2_r, q_s, q_r, ex_s, ex_r):
    row, col = lax.axis_index("row"), lax.axis_index("col")
    y, x = col // SIDE, col % SIDE
    n_z = n_row // 2
    z, core = row // 2, row % 2
    share, depth = tok.shape
    rank = ain.shape[1]
    width = aout.shape[2]
    fq = width // SIDE
    tb = share * n_row // SIDE
    rq = rank // SIDE
    own_rows = tb // SIDE
    half = tb // 2
    top, bottom = pl.ds(0, half), pl.ds(half, half)
    first, second = (x, y), (y, x)

    def wrap(v):
        return (v + 2 * SIDE) % SIDE

    def at_x(k):
        return (row, y * SIDE + wrap(x + k))

    def at_y(k):
        return (row, wrap(y + k) * SIDE + x)

    def at_row(k):
        return ((row + k) % n_row, col)

    def at_core():
        return (z * 2 + (1 - core), col)

    def at_z(k):
        return (((z + k) % n_z) * 2 + core, col)

    ring1 = (at_x, at_y)
    ring2 = (at_y, at_x)

    def quarter(q):
        return pl.ds(pl.multiple_of(q * fq, 128), fq)

    def offset(m):
        return (2 - m + 3 * ((m * (m - 1)) // 2) + 8) % SIDE

    barrier = pltpu.get_barrier_semaphore()
    peers = [at_x(k) for k in (1, 2, 3)] + [at_y(k) for k in (1, 2, 3)]
    peers += [at_row(k) for k in range(1, n_row)]
    for peer in peers:
        pl.semaphore_signal(barrier, inc=1, device_id=peer, device_id_type=MESH)

    def own_tokens():
        return lhs.at[pl.ds(pl.multiple_of(row * share, 16), share), :]

    loads = [
        pltpu.make_async_copy(ain, ainv, in_sem.at[0]),
        pltpu.make_async_copy(aout, aoutv, in_sem.at[1]),
        pltpu.make_async_copy(tok, own_tokens(), in_sem.at[2]),
        pltpu.make_async_copy(mag, magv, in_sem.at[3]),
        pltpu.make_async_copy(cot.at[:, quarter(x)], cotq.at[x], in_sem.at[4]),
    ]

    def w_copy(p, q):
        return pltpu.make_async_copy(
            w_hbm.at[p, :, quarter(q)], wb.at[p, q], w_sem.at[p * SIDE + q])

    loads[0].start()
    loads[1].start()
    for p in range(2):
        w_copy(p, wrap(x + ORDER[0])).start()
    for c in loads[2:]:
        c.start()
    for j in ORDER[1:]:
        for p in range(2):
            w_copy(p, wrap(x + j)).start()

    def remote(src, dst, send, recv, peer):
        return pltpu.make_async_remote_copy(
            src_ref=src, dst_ref=dst, send_sem=send, recv_sem=recv,
            device_id=peer, device_id_type=MESH)

    def tok_rows(owner):
        return lhs.at[pl.ds(pl.multiple_of(owner * share, 16), share), :]

    def tok_copy(i):
        if i == 0:
            owner, peer = row, at_core()
        elif i < n_z:
            owner, peer = row, at_z(i)
        else:
            owner = ((z + n_z - (i - n_z + 1)) % n_z) * 2 + core
            peer = at_core()
        return remote(tok_rows(owner), tok_rows(owner), tok_s.at[i], tok_r.at[i], peer)

    n_tok = 2 * n_z - 1
    z_order = [1, n_z - 1] + list(range(2, n_z - 1))

    def exchange(e, peer_of, count, src, dst):
        return [remote(src(k), dst(k), ex_s.at[e * 8 + k], ex_r.at[e * 8 + k], peer_of(k))
                for k in range(1, count)]

    started = []

    def begin(copies):
        for c in copies:
            c.start()
        started.extend(copies)
        return copies

    def arrive(copies):
        for c in copies:
            c.wait_recv()

    def q_first(p, k, j):
        if p == 0:
            src, dst, i = qq.at[0, wrap(x + k)], qr.at[0, k], k
        else:
            q = wrap(x + j)
            src, dst, i = qq.at[1, wrap(y + k), q], qr.at[1, k, q], SIDE + k * SIDE + j
        return remote(src, dst, q_s.at[i], q_r.at[i], ring1[p](k))

    for i in range(2):
        loads[i].wait()
    for p in range(2):
        ain_t[p] = ainv[p].astype(F32).T.astype(BF16)
    step = min(128, depth)

    def prepare(m):
        q = wrap(x + offset(m))
        for p in range(2):
            w_copy(p, q).wait()
            left = aoutv[p, :, quarter(q)]

            def body(i, acc):
                rows = pl.ds(pl.multiple_of(i * step, step), step)
                low = jnp.dot(ain_t[p, rows, :], left, preferred_element_type=F32)
                d = wb[p, q, rows, :].astype(F32) + low
                wb[p, q, rows, :] = d.astype(BF16)
                return acc + jnp.sum((d * d).reshape(step // 8, 8, fq), axis=0)

            acc = lax.fori_loop(0, depth // step, body, jnp.zeros((8, fq), F32))
            ssb[q, p:p + 1, :] = jnp.sum(acc, axis=0, keepdims=True)
            res = jnp.dot(ainv[p], wb[p, q], preferred_element_type=F32).astype(BF16)
            for b in range(SIDE):
                piece = res[b * rq:(b + 1) * rq, :]
                if p == 0:
                    qq[0, q, b] = piece
                else:
                    qq[1, b, q] = piece

    def q_send(m):
        j = offset(m)

        @pl.when(m < SIDE - 1)
        def _():
            q_first(0, j, 0).start()

        for k in (2, 1, 3):
            q_first(1, k, j).start()

    def early(m, carry):
        prepare(m)
        return carry

    lax.fori_loop(0, 2, early, 0)

    pl.semaphore_wait(barrier, len(peers))
    loads[2].wait()
    for i in z_order + [0]:
        tok_copy(i).start()
    cot_x = begin(exchange(0, at_x, SIDE, lambda k: cot.at[:, quarter(wrap(x + k))],
                           lambda k: cotq.at[x]))

    def early_send(m, carry):
        q_send(m)
        return carry

    lax.fori_loop(0, 2, early_send, 0)

    def later(m, carry):
        prepare(m)
        q_send(m)
        return carry

    lax.fori_loop(2, SIDE, later, 0)
    ss_x = begin(exchange(1, at_x, SIDE, lambda k: ssb.at[wrap(x + k)], lambda k: ssr.at[k]))

    for i in z_order:
        tok_copy(i).wait_recv()
        tok_copy(n_z - 1 + i).start()
    tok_copy(0).wait_recv()
    for i in range(n_z, n_tok):
        tok_copy(i).wait_recv()

    def product(p, q):
        res = jnp.dot(lhs[...], wb[p, q], preferred_element_type=F32).astype(BF16)
        for b in range(SIDE):
            piece = res[b * tb:(b + 1) * tb, :]
            if p == 0:
                pp[0, q, b] = piece
            else:
                pp[1, b, q] = piece

    def main_copy(p, d, kind, j):
        c1, s = first[p], wrap(second[p] + j)
        peer = ring1[p](1 if d == 0 else -1)
        if kind == FAR:
            rows = top if d == 0 else bottom
            src = pp.at[p, wrap(c1 + 2), s, rows, :]
            dst = rfar.at[p, j, rows, :]
        else:
            rows = top if (d == 0) == (kind == ACC) else bottom
            src = pp.at[p, wrap(c1 + (1 if d == 0 else -1)), s, rows, :]
            dst = rnear.at[p, d, j, rows, :]
        i = ((p * 2 + d) * 3 + kind) * SIDE + j
        return remote(src, dst, main_s.at[i], main_r.at[i], peer)

    def ph2_copy(p, d, kind):
        c1, c2 = first[p], second[p]
        peer = ring2[p](1 if d == 0 else -1)
        if kind == FAR:
            rows = top if d == 0 else bottom
            src = pp.at[p, c1, wrap(c2 + 2), rows, :]
            dst = sfar.at[p, rows, :]
        else:
            rows = top if (d == 0) == (kind == ACC) else bottom
            src = pp.at[p, c1, wrap(c2 + (1 if d == 0 else -1)), rows, :]
            dst = snear.at[p, d, rows, :]
        i = (p * 2 + d) * 3 + kind
        return remote(src, dst, ph2_s.at[i], ph2_r.at[i], peer)

    z_y = exchange(3, at_y, SIDE, lambda k: zb.at[wrap(y + k)], lambda k: zr.at[k])

    def stage(i_p, carry):
        j_p = offset(i_p)
        q = wrap(x + j_p)
        product(0, q)

        @pl.when(i_p == 0)
        def _():
            for j in ORDER:
                for d in range(2):
                    main_copy(0, d, FAR, j).start()

        @pl.when(i_p == 1)
        def _():
            for j in ORDER[:3]:
                main_copy(0, 0, RAW, j).start()

        @pl.when(i_p == 2)
        def _():
            for j in ORDER[:3]:
                main_copy(0, 1, RAW, j).start()

        product(1, q)
        for d in range(2):
            main_copy(1, d, FAR, j_p).start()

        @pl.when(i_p < 3)
        def _():
            for d in range(2):
                main_copy(1, d, RAW, j_p).start()

        @pl.when(i_p == 0)
        def _():
            ain_all = ainv[...].reshape(2 * rank, depth)
            for b in range(SIDE):
                zb[b] = nt_dot(ain_all, lhs[b * tb:(b + 1) * tb, :]).astype(BF16)
            for c in z_y:
                c.start()

        return carry

    lax.fori_loop(0, SIDE, stage, 0)

    def add_into(dst, src):
        dst[...] = (dst[...].astype(F32) + src[...].astype(F32)).astype(BF16)

    def accumulate(j):
        for p in range(2):
            for d in range(2):
                main_copy(p, d, FAR, j).wait_recv()
                rows = top if d == 0 else bottom
                near = wrap(first[p] + (1 if d == 0 else -1))
                add_into(pp.at[p, near, wrap(second[p] + j), rows, :], rfar.at[p, j, rows, :])

    for j in ORDER[:3]:
        accumulate(j)
        for p in range(2):
            for d in range(2):
                main_copy(p, d, ACC, j).start()

    arrive(ss_x)
    ssx[...] = ssb[x] + ssr[1] + ssr[2] + ssr[3]
    ss_y = begin(exchange(2, at_y, SIDE, lambda k: ssx, lambda k: ssr2.at[k]))
    arrive(z_y)
    zx[...] = (zb[y].astype(F32) + zr[1].astype(F32) + zr[2].astype(F32)
               + zr[3].astype(F32)).astype(BF16)
    z_x = begin(exchange(4, at_x, SIDE, lambda k: zx, lambda k: zr2.at[k]))
    for k in (2, 1, 3):
        q_first(0, k, 0).wait_recv()
    for j in ORDER:
        for k in (2, 1, 3):
            q_first(1, k, j).wait_recv()
    q_two = []
    for p in range(2):
        qx[p] = (qq[p, first[p]].astype(F32) + qr[p, 1].astype(F32) + qr[p, 2].astype(F32)
                 + qr[p, 3].astype(F32)).astype(BF16)
        q_two.append(begin(exchange(
            17 + p, ring2[p], SIDE, lambda k, p=p: qx.at[p, wrap(second[p] + k)],
            lambda k, p=p: qr2.at[p, k])))

    def finish(j):
        for p in range(2):
            for d in range(2):
                main_copy(p, d, RAW, j).wait_recv()
                main_copy(p, d, ACC, j).wait_recv()
            mine = pp.at[p, first[p], wrap(second[p] + j)]
            mine[...] = (mine[...].astype(F32) + rnear[p, 0, j].astype(F32)
                         + rnear[p, 1, j].astype(F32)).astype(BF16)

    finish(2)
    for p in range(2):
        for d in range(2):
            ph2_copy(p, d, FAR).start()
    finish(1)
    for p in range(2):
        ph2_copy(p, 0, RAW).start()
    finish(3)
    for p in range(2):
        ph2_copy(p, 1, RAW).start()
    for p in range(2):
        for d in range(2):
            main_copy(p, d, RAW, 0).start()
    accumulate(0)
    for p in range(2):
        for d in range(2):
            ph2_copy(p, d, FAR).wait_recv()
            rows = top if d == 0 else bottom
            near = wrap(second[p] + (1 if d == 0 else -1))
            add_into(pp.at[p, first[p], near, rows, :], sfar.at[p, rows, :])
            ph2_copy(p, d, ACC).start()
    for p in range(2):
        for d in range(2):
            main_copy(p, d, ACC, 0).start()
    arrive(ss_y)
    total = ssx[...] + ssr2[1] + ssr2[2] + ssr2[3]
    norm = jnp.sqrt(total + EPSILON)
    loads[3].wait()
    mag_q = magv[:, quarter(x)]
    coef = mag_q / norm
    arrive(z_x)
    zs[...] = (zx[...].astype(F32) + zr2[1].astype(F32) + zr2[2].astype(F32)
               + zr2[3].astype(F32)).astype(BF16)
    arrive(cot_x)
    loads[4].wait()

    finish(0)
    for p in range(2):
        for d in range(2):
            ph2_copy(p, d, RAW).wait_recv()
            ph2_copy(p, d, ACC).wait_recv()

    def summed(p, rows):
        return (pp[p, first[p], second[p], rows, :].astype(F32)
                + snear[p, 0, rows, :].astype(F32) + snear[p, 1, rows, :].astype(F32))

    coef0, coef1 = coef[0:1], coef[1:2]
    chunk = min(16, own_rows)
    per = own_rows // chunk

    def gating(i, carry):
        acc0, acc1 = carry
        rows = pl.ds(pl.multiple_of(i * chunk, chunk), chunk)
        inner = pl.ds(pl.multiple_of((i % per) * chunk, chunk), chunk)
        raw0, raw1 = summed(0, rows), summed(1, rows)
        gate, up = raw0 * coef0, raw1 * coef1
        sig = jax.nn.sigmoid(gate)
        hidq[i // per, inner, :] = (gate * sig * up).astype(BF16)
        c = cotq[i // per, inner, :].astype(F32)
        d0 = (c * up * sig * (1.0 + gate * (1.0 - sig))).astype(BF16)
        d1 = (c * gate * sig).astype(BF16)
        dsc[0, rows, :] = d0
        dsc[1, rows, :] = d1
        s0 = jnp.sum((d0.astype(F32) * raw0).reshape(chunk // 8, 8, fq), axis=0)
        s1 = jnp.sum((d1.astype(F32) * raw1).reshape(chunk // 8, 8, fq), axis=0)
        return (acc0 + s0, acc1 + s1)

    zero = jnp.zeros((8, fq), F32)
    acc0, acc1 = lax.fori_loop(0, tb // chunk, gating, (zero, zero))
    st[0:1] = jnp.sum(acc0, axis=0, keepdims=True)
    st[1:2] = jnp.sum(acc1, axis=0, keepdims=True)
    st_y = begin(exchange(6, at_y, SIDE, lambda k: st, lambda k: strr.at[k]))

    for p in range(2):
        scaled = (aoutv[p, :, quarter(x)].astype(F32) * coef[p:p + 1]).astype(BF16)
        wv[p * rank:(p + 1) * rank, :] = nt_dot(scaled, dsc[p]).astype(BF16)
    w_x = begin(exchange(9, at_x, SIDE, lambda k: wv, lambda k: wr.at[k]))
    for p in range(2):
        res = jnp.dot(zs[p * rank:(p + 1) * rank, :], dsc[p], preferred_element_type=F32)
        for b in range(SIDE):
            g1[b, p] = res[b * rq:(b + 1) * rq, :].astype(BF16)
    g1_y = begin(exchange(8, at_y, SIDE, lambda k: g1.at[wrap(y + k)], lambda k: g1r.at[k]))
    hid_x = begin(exchange(5, at_x, SIDE, lambda k: hidq.at[wrap(x + k)], lambda k: hidr.at[x]))
    hidr[x] = hidq[x]

    arrive(st_y)
    stat = st[...] + strr[1] + strr[2] + strr[3]
    tilt = mag_q * stat / (norm * norm * norm)
    bb[0:2] = tilt
    bb[2:4] = stat / norm
    b_x = begin(exchange(7, at_x, SIDE, lambda k: bb, lambda k: ball.at[x]))
    ball[x] = bb[...]

    arrive(w_x)
    wx[...] = (wv[...].astype(F32) + wr[1].astype(F32) + wr[2].astype(F32)
               + wr[3].astype(F32)).astype(BF16)
    w_y = begin(exchange(10, at_y, SIDE, lambda k: wx, lambda k: wall.at[y]))
    wall[y] = wx[...]

    arrive(g1_y)
    for p in range(2):
        arrive(q_two[p])
        both = (g1[y, p].astype(F32) + g1r[1, p].astype(F32) + g1r[2, p].astype(F32)
                + g1r[3, p].astype(F32))
        low = (qx[p, second[p]].astype(F32) + qr2[p, 1].astype(F32) + qr2[p, 2].astype(F32)
               + qr2[p, 3].astype(F32))
        gall[p, second[p], first[p]] = (coef[p:p + 1] * both - tilt[p:p + 1] * low).astype(BF16)
    ga_x = begin(exchange(11, at_x, SIDE, lambda k: gall.at[0, y, x], lambda k: gall.at[0, y, x]))
    gb_y = begin(exchange(13, at_y, SIDE, lambda k: gall.at[1, x, y], lambda k: gall.at[1, x, y]))

    def tilted(p, q, b):
        scaled = (aoutv[p, :, quarter(q)].astype(F32) * b).astype(BF16)
        return nt_dot(scaled, wb[p, q])

    for p in range(2):
        tin[p] = -tilted(p, x, tilt[p:p + 1])

    arrive(w_y)
    for p in range(2):
        t1 = tin[p]
        for b in range(SIDE):
            t1 = t1 + jnp.dot(wall[b, p * rank:(p + 1) * rank, :], lhs[b * tb:(b + 1) * tb, :],
                              preferred_element_type=F32)
        tin[p] = t1

    arrive(b_x)
    out_rows = 2 * rank // n_row
    for p in range(2):
        t1 = tin[p]
        for k in range(1, SIDE):
            q = wrap(x + k)
            t1 = t1 - tilted(p, q, ball[q, p:p + 1])
        for b in range(rank // out_rows):
            gib[p * (rank // out_rows) + b] = t1[b * out_rows:(b + 1) * out_rows].astype(BF16)
    gi_rs = begin(exchange(15, at_row, n_row, lambda k: gib.at[(row + k) % n_row],
                           lambda k: gir.at[k]))

    arrive(ga_x)
    ga_y = begin(exchange(12, at_y, SIDE, lambda k: gall.at[0, y], lambda k: gall.at[0, y]))
    arrive(gb_y)
    gb_x = begin(exchange(14, at_x, SIDE, lambda k: gall.at[1, x], lambda k: gall.at[1, x]))
    for q in range(SIDE):
        gmq[q] = ball[q, 2:4, :]
    arrive(hid_x)
    outs = [
        pltpu.make_async_copy(gmq, gm_out, out_sem.at[0]),
        pltpu.make_async_copy(hidr, hid_out, out_sem.at[1]),
        pltpu.make_async_copy(gall, go_out, out_sem.at[2]),
        pltpu.make_async_copy(giall, gi_out, out_sem.at[3]),
    ]
    outs[0].start()
    outs[1].start()

    arrive(gi_rs)
    acc = gib[row].astype(F32)
    for k in range(1, n_row):
        acc = acc + gir[k].astype(F32)
    gio[...] = acc.astype(BF16)
    gi_ag = begin(exchange(16, at_row, n_row, lambda k: gio, lambda k: giall.at[row]))
    giall[row] = gio[...]

    arrive(ga_y)
    arrive(gb_x)
    outs[2].start()
    arrive(gi_ag)
    outs[3].start()

    for i in range(n_tok):
        tok_copy(i).wait_send()
    for c in z_y:
        c.wait_send()
    for k in (1, 2, 3):
        q_first(0, k, 0).wait_send()
        for j in range(SIDE):
            q_first(1, k, j).wait_send()
    for p in range(2):
        for d in range(2):
            for kind in range(3):
                for j in range(SIDE):
                    main_copy(p, d, kind, j).wait_send()
                ph2_copy(p, d, kind).wait_send()
    for c in started:
        c.wait_send()
    for c in outs:
        c.wait()


def finish_kernel(hidr, giall, gall, gmq, hid, gi, go, gm):
    fq = hidr.shape[2]
    rq = gall.shape[3]
    n_row, out_rows = giall.shape[:2]
    per = n_row // 2
    for q in range(SIDE):
        lanes = slice(q * fq, (q + 1) * fq)
        hid[:, lanes] = hidr[q]
        gm[:, lanes] = gmq[q]
        for b in range(SIDE):
            go[0, b * rq:(b + 1) * rq, lanes] = gall[0, b, q].astype(F32)
            go[1, b * rq:(b + 1) * rq, lanes] = gall[1, q, b].astype(F32)
    for p in range(2):
        for b in range(per):
            gi[p, b * out_rows:(b + 1) * out_rows, :] = giall[p * per + b].astype(F32)


def solution(mesh):
    n_row = mesh.shape["row"]

    def on_device(tokens, weights, adapter_in, adapter_out, magnitude, hidden_cot):
        share, depth = tokens.shape
        rank = adapter_in.shape[1]
        width = adapter_out.shape[2]
        fq = width // SIDE
        tb = share * n_row // SIDE
        rq = rank // SIDE
        own_rows = tb // SIDE
        pr = 2 * rank
        vm = pltpu.VMEM
        dma = pltpu.SemaphoreType.DMA
        scratch = [
            vm((SIDE * tb, depth), BF16),
            vm((2, SIDE, depth, fq), BF16),
            vm((2, SIDE, SIDE, tb, fq), BF16),
            vm((2, rank, depth), BF16),
            vm((2, rank, width), BF16),
            vm((2, width), F32),
            vm((2, depth, rank), BF16),
            vm((2, SIDE, tb, fq), BF16),
            vm((2, 2, SIDE, tb, fq), BF16),
            vm((2, tb, fq), BF16),
            vm((2, 2, tb, fq), BF16),
            vm((SIDE, own_rows, fq), BF16),
            vm((SIDE, 2, fq), F32),
            vm((2, fq), F32),
            vm((SIDE, 2, fq), F32),
            vm((SIDE, 2, fq), F32),
            vm((SIDE, pr, tb), BF16),
            vm((pr, tb), BF16),
            vm((pr, tb), BF16),
            vm((SIDE, pr, tb), BF16),
            vm((SIDE, pr, tb), BF16),
            vm((SIDE, own_rows, fq), BF16),
            vm((SIDE, own_rows, fq), BF16),
            vm((2, tb, fq), BF16),
            vm((2, fq), F32),
            vm((SIDE, 2, fq), F32),
            vm((4, fq), F32),
            vm((SIDE, 4, fq), F32),
            vm((SIDE, 2, fq), F32),
            vm((SIDE, 2, rq, fq), BF16),
            vm((SIDE, 2, rq, fq), BF16),
            vm((pr, tb), BF16),
            vm((pr, tb), BF16),
            vm((SIDE, pr, tb), BF16),
            vm((SIDE, pr, tb), BF16),
            vm((2, SIDE, SIDE, rq, fq), BF16),
            vm((2, SIDE, SIDE, rq, fq), BF16),
            vm((2, SIDE, rq, fq), BF16),
            vm((2, SIDE, rq, fq), BF16),
            vm((2, SIDE, SIDE, rq, fq), BF16),
            vm((n_row, pr // n_row, depth), BF16),
            vm((n_row, pr // n_row, depth), BF16),
            vm((pr // n_row, depth), BF16),
            vm((n_row, pr // n_row, depth), BF16),
            vm((2, rank, depth), F32),
            dma((2 * SIDE,)),
            dma((5,)),
            dma((4,)),
            dma((n_row,)),
            dma((n_row,)),
            dma((12 * SIDE,)),
            dma((12 * SIDE,)),
            dma((12,)),
            dma((12,)),
            dma((5 * SIDE,)),
            dma((5 * SIDE,)),
            dma((EXCHANGES * 8,)),
            dma((EXCHANGES * 8,)),
        ]
        anywhere = pl.BlockSpec(memory_space=pl.ANY)
        parts = pl.pallas_call(
            functools.partial(kernel, n_row),
            out_shape=(
                jax.ShapeDtypeStruct((SIDE, own_rows, fq), BF16),
                jax.ShapeDtypeStruct((n_row, pr // n_row, depth), BF16),
                jax.ShapeDtypeStruct((2, SIDE, SIDE, rq, fq), BF16),
                jax.ShapeDtypeStruct((SIDE, 2, fq), F32),
            ),
            in_specs=[anywhere] * 6,
            out_specs=(anywhere,) * 4,
            scratch_shapes=scratch,
            compiler_params=pltpu.CompilerParams(
                collective_id=0, has_side_effects=True, vmem_limit_bytes=67_043_328
            ),
        )(tokens, weights, adapter_in, adapter_out, magnitude, hidden_cot)
        return pl.pallas_call(
            finish_kernel,
            out_shape=(
                jax.ShapeDtypeStruct(hidden_cot.shape, BF16),
                jax.ShapeDtypeStruct(adapter_in.shape, F32),
                jax.ShapeDtypeStruct(adapter_out.shape, F32),
                jax.ShapeDtypeStruct(magnitude.shape, F32),
            ),
        )(*parts)

    in_specs = (
        P("row", "col"),
        P(None, "col", "row"),
        P(None, None, "col"),
        P(None, None, "row"),
        P(None, "row"),
        P("col", "row"),
    )
    out_specs = (P("col", "row"), P(None, None, "col"), P(None, None, "row"), P(None, "row"))
    return jax.shard_map(
        on_device, mesh=mesh, in_specs=in_specs, out_specs=out_specs, check_vma=False
    )
```

```python
import functools

import jax
import jax.numpy as jnp
from jax import lax
from jax.experimental import pallas as pl
from jax.experimental.pallas import tpu as pltpu
from jax.sharding import PartitionSpec as P

EPSILON = 1e-06
F32 = jnp.float32
BF16 = jnp.bfloat16
MESH = pl.DeviceIdType.MESH
SIDE = 4
ORDER = (2, 1, 3, 0)
EXCHANGES = 19
FAR, RAW, ACC = 0, 1, 2


def nt_dot(a, b):
    return lax.dot_general(a, b, (((1,), (1,)), ((), ())), preferred_element_type=F32)


def kernel(n_row, tok, w_hbm, ain, aout, mag, cot, hid_out, gi_out, go_out, gm_out,
           lhs, wb, pp, ainv, aoutv, magv, ain_t, rfar, rnear, sfar, snear, cotq, ssb, ssx, ssr, ssr2,
           zb, zx, zs, zr, zr2, hidq, hidr, dsc, st, strr, bb, ball, gmq, g1, g1r,
           wv, wx, wr, wall, qq, qr, qx, qr2, gall, gib, gir, gio, giall, tin,
           w_sem, a_sem, in_sem, out_sem, hid_sem, gat_s, gat_r, tok_s, tok_r, main_s, main_r, ph2_s, ph2_r, q_s, q_r, ex_s, ex_r):
    row, col = lax.axis_index("row"), lax.axis_index("col")
    y, x = col // SIDE, col % SIDE
    n_z = n_row // 2
    z, core = row // 2, row % 2
    share, depth = tok.shape
    rank = ain.shape[1]
    width = aout.shape[2]
    fq = width // SIDE
    tb = share * n_row // SIDE
    rq = rank // SIDE
    own_rows = tb // SIDE
    half = tb // 2
    top, bottom = pl.ds(0, half), pl.ds(half, half)
    first, second = (x, y), (y, x)

    def wrap(v):
        return (v + 2 * SIDE) % SIDE

    def at_x(k):
        return (row, y * SIDE + wrap(x + k))

    def at_y(k):
        return (row, wrap(y + k) * SIDE + x)

    def at_row(k):
        return ((row + k) % n_row, col)

    def at_core():
        return (z * 2 + (1 - core), col)

    def at_z(k):
        return (((z + k) % n_z) * 2 + core, col)

    ring1 = (at_x, at_y)
    ring2 = (at_y, at_x)

    def quarter(q):
        return pl.ds(pl.multiple_of(q * fq, 128), fq)

    def offset(m):
        return (2 - m + 3 * ((m * (m - 1)) // 2) + 8) % SIDE

    barrier = pltpu.get_barrier_semaphore()
    peers = [at_x(k) for k in (1, 2, 3)] + [at_y(k) for k in (1, 2, 3)]
    peers += [at_row(k) for k in range(1, n_row)]
    for peer in peers:
        pl.semaphore_signal(barrier, inc=1, device_id=peer, device_id_type=MESH)

    def own_tokens():
        return lhs.at[pl.ds(pl.multiple_of(row * share, 16), share), :]

    loads = [
        pltpu.make_async_copy(ain, ainv, in_sem.at[0]),
        pltpu.make_async_copy(tok, own_tokens(), in_sem.at[1]),
        pltpu.make_async_copy(mag, magv, in_sem.at[2]),
        pltpu.make_async_copy(cot.at[:, quarter(x)], cotq.at[x], in_sem.at[3]),
    ]

    def w_copy(p, q):
        return pltpu.make_async_copy(
            w_hbm.at[p, :, quarter(q)], wb.at[p, q], w_sem.at[p * SIDE + q])

    def out_copy(q):
        return pltpu.make_async_copy(aout.at[:, :, quarter(q)], aoutv.at[q], a_sem.at[q])

    loads[1].start()
    loads[0].start()
    for j in ORDER:
        out_copy(wrap(x + j)).start()
        for p in range(2):
            w_copy(p, wrap(x + j)).start()
        if j == ORDER[0]:
            for c in loads[2:]:
                c.start()

    def remote(src, dst, send, recv, peer):
        return pltpu.make_async_remote_copy(
            src_ref=src, dst_ref=dst, send_sem=send, recv_sem=recv,
            device_id=peer, device_id_type=MESH)

    def tok_rows(owner):
        return lhs.at[pl.ds(pl.multiple_of(owner * share, 16), share), :]

    def tok_copy(i):
        if i == 0:
            owner, peer = row, at_core()
        elif i < n_z:
            owner, peer = row, at_z(i)
        else:
            owner = ((z + n_z - (i - n_z + 1)) % n_z) * 2 + core
            peer = at_core()
        return remote(tok_rows(owner), tok_rows(owner), tok_s.at[i], tok_r.at[i], peer)

    n_tok = 2 * n_z - 1
    z_order = [1, n_z - 1] + list(range(2, n_z - 1))

    def peers_of(count):
        return (2, 1, 3) if count == SIDE else range(1, count)

    def exchange(e, peer_of, count, src, dst):
        return [remote(src(k), dst(k), ex_s.at[e * 8 + k], ex_r.at[e * 8 + k], peer_of(k))
                for k in peers_of(count)]

    started = []

    def begin(copies):
        for c in copies:
            c.start()
        started.extend(copies)
        return copies

    def arrive(copies):
        for c in copies:
            c.wait_recv()

    def q_first(p, k, j):
        if p == 0:
            src, dst, i = qq.at[0, wrap(x + k)], qr.at[0, k], k
        else:
            q = wrap(x + j)
            src, dst, i = qq.at[1, wrap(y + k), q], qr.at[1, k, q], SIDE + k * SIDE + j
        return remote(src, dst, q_s.at[i], q_r.at[i], ring1[p](k))

    cot_x = exchange(0, at_x, SIDE, lambda k: cot.at[:, quarter(wrap(x + k))], lambda k: cotq.at[x])

    pl.semaphore_wait(barrier, len(peers))
    loads[1].wait()
    for i in z_order + [0]:
        tok_copy(i).start()
    for c in cot_x:
        c.start()

    loads[0].wait()
    for p in range(2):
        ain_t[p] = ainv[p].astype(F32).T.astype(BF16)
    step = min(128, depth)

    def prepare(m):
        q = wrap(x + offset(m))
        out_copy(q).wait()
        for p in range(2):
            w_copy(p, q).wait()
            left = aoutv[q, p]

            def body(i, acc):
                rows = pl.ds(pl.multiple_of(i * step, step), step)
                low = jnp.dot(ain_t[p, rows, :], left, preferred_element_type=F32)
                d = wb[p, q, rows, :].astype(F32) + low
                wb[p, q, rows, :] = d.astype(BF16)
                return acc + jnp.sum((d * d).reshape(step // 8, 8, fq), axis=0)

            acc = lax.fori_loop(0, depth // step, body, jnp.zeros((8, fq), F32))
            ssb[q, p:p + 1, :] = jnp.sum(acc, axis=0, keepdims=True)
            res = jnp.dot(ainv[p], wb[p, q], preferred_element_type=F32).astype(BF16)
            for b in range(SIDE):
                piece = res[b * rq:(b + 1) * rq, :]
                if p == 0:
                    qq[0, q, b] = piece
                else:
                    qq[1, b, q] = piece

    def q_send(m):
        j = offset(m)

        if not (isinstance(m, int) and m == SIDE - 1):
            q_first(0, j, 0).start()

        for k in (2, 1, 3):
            q_first(1, k, j).start()

    def early(m, carry):
        prepare(m)
        q_send(m)

        @pl.when(m == 0)
        def _():
            for i in z_order[:2]:
                tok_copy(i).wait_recv()
                tok_copy(n_z - 1 + i).start()

        return carry

    lax.fori_loop(0, 2, early, 0)

    for i in z_order[2:]:
        tok_copy(i).wait_recv()
        tok_copy(n_z - 1 + i).start()
    tok_copy(0).wait_recv()
    for i in range(n_z, n_tok):
        tok_copy(i).wait_recv()

    def product(p, q):
        res = jnp.dot(lhs[...], wb[p, q], preferred_element_type=F32).astype(BF16)
        for b in range(SIDE):
            piece = res[b * tb:(b + 1) * tb, :]
            if p == 0:
                pp[0, q, b] = piece
            else:
                pp[1, b, q] = piece

    def main_copy(p, d, kind, j):
        c1, s = first[p], wrap(second[p] + j)
        peer = ring1[p](1 if d == 0 else -1)
        if kind == FAR:
            rows = top if d == 0 else bottom
            src = pp.at[p, wrap(c1 + 2), s, rows, :]
            dst = rfar.at[p, j, rows, :]
        else:
            rows = top if (d == 0) == (kind == ACC) else bottom
            src = pp.at[p, wrap(c1 + (1 if d == 0 else -1)), s, rows, :]
            dst = rnear.at[p, d, j, rows, :]
        i = ((p * 2 + d) * 3 + kind) * SIDE + j
        return remote(src, dst, main_s.at[i], main_r.at[i], peer)

    def ph2_copy(p, d, kind):
        c1, c2 = first[p], second[p]
        peer = ring2[p](1 if d == 0 else -1)
        if kind == FAR:
            rows = top if d == 0 else bottom
            src = pp.at[p, c1, wrap(c2 + 2), rows, :]
            dst = sfar.at[p, rows, :]
        else:
            rows = top if (d == 0) == (kind == ACC) else bottom
            src = pp.at[p, c1, wrap(c2 + (1 if d == 0 else -1)), rows, :]
            dst = snear.at[p, d, rows, :]
        i = (p * 2 + d) * 3 + kind
        return remote(src, dst, ph2_s.at[i], ph2_r.at[i], peer)

    ss_x = exchange(1, at_x, SIDE, lambda k: ssb.at[wrap(x + k)], lambda k: ssr.at[k])
    z_y = exchange(3, at_y, SIDE, lambda k: zb.at[wrap(y + k)], lambda k: zr.at[k])

    def add_into(dst, src):
        dst[...] = (dst[...].astype(F32) + src[...].astype(F32)).astype(BF16)

    def accumulate(j):
        for p in range(2):
            for d in range(2):
                main_copy(p, d, FAR, j).wait_recv()
                rows = top if d == 0 else bottom
                near = wrap(first[p] + (1 if d == 0 else -1))
                add_into(pp.at[p, near, wrap(second[p] + j), rows, :], rfar.at[p, j, rows, :])

    def send_sums(j):
        for p in range(2):
            for d in range(2):
                main_copy(p, d, ACC, j).start()

    def finish(p, j):
        for d in range(2):
            main_copy(p, d, RAW, j).wait_recv()
            main_copy(p, d, ACC, j).wait_recv()
        mine = pp.at[p, first[p], wrap(second[p] + j)]
        mine[...] = (mine[...].astype(F32) + rnear[p, 0, j].astype(F32)
                     + rnear[p, 1, j].astype(F32)).astype(BF16)

    def second_sum(p, d):
        ph2_copy(p, d, FAR).wait_recv()
        rows = top if d == 0 else bottom
        near = wrap(second[p] + (1 if d == 0 else -1))
        add_into(pp.at[p, first[p], near, rows, :], sfar.at[p, rows, :])
        ph2_copy(p, d, ACC).start()

    def stage(i_p, carry):
        j_p = offset(i_p)
        q = wrap(x + j_p)
        product(0, q)

        @pl.when(i_p == 0)
        def _():
            for j in ORDER:
                for d in range(2):
                    main_copy(0, d, FAR, j).start()

        @pl.when(i_p == 1)
        def _():
            for j in ORDER[:3]:
                main_copy(0, 0, RAW, j).start()

        @pl.when(i_p == 2)
        def _():
            for j in ORDER[:3]:
                main_copy(0, 1, RAW, j).start()

        product(1, q)
        for d in range(2):
            main_copy(1, d, FAR, j_p).start()

        @pl.when(i_p < 3)
        def _():
            for d in range(2):
                main_copy(1, d, RAW, j_p).start()

        @pl.when(i_p < 2)
        def _():
            prepare(i_p + 2)

            @pl.when(i_p == 1)
            def _():
                for c in ss_x:
                    c.start()

        @pl.when(i_p == 2)
        def _():
            accumulate(2)
            send_sums(2)

        @pl.when(i_p == 3)
        def _():
            accumulate(1)
            send_sums(1)

        return carry

    lax.fori_loop(0, SIDE, stage, 0)

    accumulate(3)
    send_sums(3)
    ain_all = ainv[...].reshape(2 * rank, depth)
    for b in range(SIDE):
        zb[b] = nt_dot(ain_all, lhs[b * tb:(b + 1) * tb, :]).astype(BF16)
    for c in z_y:
        c.start()
    accumulate(0)

    for p in range(2):
        finish(p, 2)
        for d in range(2):
            ph2_copy(p, d, FAR).start()
    for p in range(2):
        for d in range(2):
            main_copy(p, d, RAW, 0).start()
    for p in range(2):
        finish(p, 1)
        ph2_copy(p, 0, RAW).start()
    arrive(ss_x)
    ssx[...] = ssb[x] + ssr[1] + ssr[2] + ssr[3]
    ss_y = begin(exchange(2, at_y, SIDE, lambda k: ssx, lambda k: ssr2.at[k]))
    for p in range(2):
        second_sum(p, 0)
    for p in range(2):
        finish(p, 3)
        ph2_copy(p, 1, RAW).start()
    for p in range(2):
        second_sum(p, 1)
    for p in range(2):
        for d in range(2):
            main_copy(p, d, ACC, 0).start()
    arrive(z_y)
    zx[...] = (zb[y].astype(F32) + zr[1].astype(F32) + zr[2].astype(F32)
               + zr[3].astype(F32)).astype(BF16)
    z_x = begin(exchange(4, at_x, SIDE, lambda k: zx, lambda k: zr2.at[k]))
    q_send(2)
    q_send(3)
    arrive(ss_y)
    total = ssx[...] + ssr2[1] + ssr2[2] + ssr2[3]
    norm = jnp.sqrt(total + EPSILON)
    loads[2].wait()
    mag_q = magv[:, quarter(x)]
    coef = mag_q / norm
    arrive(cot_x)
    loads[3].wait()

    for p in range(2):
        finish(p, 0)
    for p in range(2):
        for d in range(2):
            ph2_copy(p, d, RAW).wait_recv()
            ph2_copy(p, d, ACC).wait_recv()

    def summed(p, rows):
        return (pp[p, first[p], second[p], rows, :].astype(F32)
                + snear[p, 0, rows, :].astype(F32) + snear[p, 1, rows, :].astype(F32))

    coef0, coef1 = coef[0:1], coef[1:2]
    chunk = min(16, own_rows)
    per = own_rows // chunk

    def gating(i, carry):
        acc0, acc1 = carry
        rows = pl.ds(pl.multiple_of(i * chunk, chunk), chunk)
        inner = pl.ds(pl.multiple_of((i % per) * chunk, chunk), chunk)
        raw0, raw1 = summed(0, rows), summed(1, rows)
        gate, up = raw0 * coef0, raw1 * coef1
        sig = jax.nn.sigmoid(gate)
        hidq[i // per, inner, :] = (gate * sig * up).astype(BF16)
        c = cotq[i // per, inner, :].astype(F32)
        d0 = (c * up * sig * (1.0 + gate * (1.0 - sig))).astype(BF16)
        d1 = (c * gate * sig).astype(BF16)
        dsc[0, rows, :] = d0
        dsc[1, rows, :] = d1
        s0 = jnp.sum((d0.astype(F32) * raw0).reshape(chunk // 8, 8, fq), axis=0)
        s1 = jnp.sum((d1.astype(F32) * raw1).reshape(chunk // 8, 8, fq), axis=0)
        return (acc0 + s0, acc1 + s1)

    zero = jnp.zeros((8, fq), F32)
    acc0, acc1 = lax.fori_loop(0, tb // chunk, gating, (zero, zero))
    st[0:1] = jnp.sum(acc0, axis=0, keepdims=True)
    st[1:2] = jnp.sum(acc1, axis=0, keepdims=True)
    st_y = begin(exchange(6, at_y, SIDE, lambda k: st, lambda k: strr.at[k]))

    for p in range(2):
        scaled = (aoutv[x, p].astype(F32) * coef[p:p + 1]).astype(BF16)
        wv[p * rank:(p + 1) * rank, :] = nt_dot(scaled, dsc[p]).astype(BF16)
    w_x = begin(exchange(9, at_x, SIDE, lambda k: wv, lambda k: wr.at[k]))
    arrive(z_x)
    zs[...] = (zx[...].astype(F32) + zr2[1].astype(F32) + zr2[2].astype(F32)
               + zr2[3].astype(F32)).astype(BF16)
    for p in range(2):
        res = jnp.dot(zs[p * rank:(p + 1) * rank, :], dsc[p], preferred_element_type=F32)
        for b in range(SIDE):
            g1[b, p] = res[b * rq:(b + 1) * rq, :].astype(BF16)
    g1_y = begin(exchange(8, at_y, SIDE, lambda k: g1.at[wrap(y + k)], lambda k: g1r.at[k]))
    hidr[x] = hidq[x]

    for k in (2, 1, 3):
        q_first(0, k, 0).wait_recv()
    for j in ORDER:
        for k in (2, 1, 3):
            q_first(1, k, j).wait_recv()
    for p in range(2):
        qx[p] = (qq[p, first[p]].astype(F32) + qr[p, 1].astype(F32) + qr[p, 2].astype(F32)
                 + qr[p, 3].astype(F32)).astype(BF16)
    q_two = [
        begin(exchange(17 + p, ring2[p], SIDE, lambda k, p=p: qx.at[p, wrap(second[p] + k)],
                       lambda k, p=p: qr2.at[p, k]))
        for p in range(2)
    ]
    arrive(st_y)
    stat = st[...] + strr[1] + strr[2] + strr[3]
    tilt = mag_q * stat / (norm * norm * norm)
    bb[0:2] = tilt
    bb[2:4] = stat / norm
    b_x = begin(exchange(7, at_x, SIDE, lambda k: bb, lambda k: ball.at[x]))
    hid_x = begin(exchange(5, at_x, SIDE, lambda k: hidq.at[wrap(x + k)], lambda k: hidr.at[x]))
    ball[x] = bb[...]

    arrive(w_x)
    wx[...] = (wv[...].astype(F32) + wr[1].astype(F32) + wr[2].astype(F32)
               + wr[3].astype(F32)).astype(BF16)
    w_y = begin(exchange(10, at_y, SIDE, lambda k: wx, lambda k: wall.at[y]))
    wall[y] = wx[...]

    arrive(g1_y)
    for p in range(2):
        arrive(q_two[p])
        both = (g1[y, p].astype(F32) + g1r[1, p].astype(F32) + g1r[2, p].astype(F32)
                + g1r[3, p].astype(F32))
        low = (qx[p, second[p]].astype(F32) + qr2[p, 1].astype(F32) + qr2[p, 2].astype(F32)
               + qr2[p, 3].astype(F32))
        gall[p, second[p], first[p]] = (coef[p:p + 1] * both - tilt[p:p + 1] * low).astype(BF16)

    def gat_one(p, k):
        piece = gall.at[p, second[p], first[p]]
        return remote(piece, piece, ex_s.at[(11 + p) * 8 + k], ex_r.at[(11 + p) * 8 + k],
                      ring1[p](k))

    def gat_two(p, i, k):
        piece = gall.at[p, second[p], wrap(first[p] - i)]
        n = (p * SIDE + i) * SIDE + k
        return remote(piece, piece, gat_s.at[n], gat_r.at[n], ring2[p](k))

    for k in (2, 1, 3):
        for p in range(2):
            gat_one(p, k).start()
    for k in (2, 1, 3):
        for p in range(2):
            gat_two(p, 0, k).start()

    def tilted(p, q, b):
        scaled = (aoutv[q, p].astype(F32) * b).astype(BF16)
        return nt_dot(scaled, wb[p, q])

    for p in range(2):
        tin[p] = -tilted(p, x, tilt[p:p + 1])

    arrive(b_x)
    out_rows = 2 * rank // n_row
    for p in range(2):
        t1 = tin[p]
        for k in range(1, SIDE):
            q = wrap(x + k)
            t1 = t1 - tilted(p, q, ball[q, p:p + 1])
        tin[p] = t1
    arrive(w_y)
    for p in range(2):
        t1 = tin[p]
        for b in range(SIDE):
            t1 = t1 + jnp.dot(wall[b, p * rank:(p + 1) * rank, :], lhs[b * tb:(b + 1) * tb, :],
                              preferred_element_type=F32)

        for b in range(rank // out_rows):
            gib[p * (rank // out_rows) + b] = t1[b * out_rows:(b + 1) * out_rows].astype(BF16)
    gi_rs = begin(exchange(15, at_row, n_row, lambda k: gib.at[(row + k) % n_row],
                           lambda k: gir.at[k]))

    for i in (1, 3, 2):
        for p in range(2):
            gat_one(p, i).wait_recv()
            for k in (2, 1, 3):
                gat_two(p, i, k).start()
    for q in range(SIDE):
        gmq[:, q * fq:(q + 1) * fq] = ball[q, 2:4, :]
    outs = [
        pltpu.make_async_copy(gmq, gm_out, out_sem.at[0]),
        pltpu.make_async_copy(giall, gi_out, out_sem.at[1]),
        pltpu.make_async_copy(gall.at[0], go_out.at[0], out_sem.at[2]),
        pltpu.make_async_copy(gall.at[1], go_out.at[1], out_sem.at[3]),
    ]
    hid_outs = [
        pltpu.make_async_copy(hidr.at[q], hid_out.at[:, q * fq:(q + 1) * fq], hid_sem.at[q])
        for q in range(SIDE)
    ]
    outs[0].start()

    arrive(gi_rs)
    acc = gib[row].astype(F32)
    for k in range(1, n_row):
        acc = acc + gir[k].astype(F32)
    gio[...] = acc.astype(BF16)
    gi_ag = begin(exchange(16, at_row, n_row, lambda k: gio, lambda k: giall.at[row]))
    giall[row] = gio[...]
    arrive(hid_x)
    for c in hid_outs:
        c.start()

    for p in range(2):
        for i in range(SIDE):
            for k in (1, 2, 3):
                gat_two(p, i, k).wait_recv()
        outs[2 + p].start()
    arrive(gi_ag)
    outs[1].start()

    for i in range(n_tok):
        tok_copy(i).wait_send()
    for c in cot_x + ss_x + z_y:
        c.wait_send()
    for p in range(2):
        for k in (1, 2, 3):
            gat_one(p, k).wait_send()
            for i in range(SIDE):
                gat_two(p, i, k).wait_send()
    for k in (1, 2, 3):
        q_first(0, k, 0).wait_send()
        for j in range(SIDE):
            q_first(1, k, j).wait_send()
    for p in range(2):
        for d in range(2):
            for kind in range(3):
                for j in range(SIDE):
                    main_copy(p, d, kind, j).wait_send()
                ph2_copy(p, d, kind).wait_send()
    for c in started:
        c.wait_send()
    for c in outs + hid_outs:
        c.wait()


def finish_kernel(hid_in, gi_in, go_in, gm_in, hid, gi, go, gm,
                  hid_v, gi_v, go_v, gm_v, gi_f, go_f, in_sem, out_sem):
    n_row, out_rows = gi_in.shape[:2]
    rq, fq = go_in.shape[3:]
    per = n_row // 2
    loads = [
        pltpu.make_async_copy(go_in.at[0], go_v.at[0], in_sem.at[0]),
        pltpu.make_async_copy(go_in.at[1], go_v.at[1], in_sem.at[1]),
        pltpu.make_async_copy(gi_in, gi_v, in_sem.at[2]),
        pltpu.make_async_copy(hid_in, hid_v, in_sem.at[3]),
        pltpu.make_async_copy(gm_in, gm_v, in_sem.at[4]),
    ]
    outs = [
        pltpu.make_async_copy(go_f.at[0], go.at[0], out_sem.at[0]),
        pltpu.make_async_copy(go_f.at[1], go.at[1], out_sem.at[1]),
        pltpu.make_async_copy(gi_f, gi, out_sem.at[2]),
        pltpu.make_async_copy(hid_v, hid, out_sem.at[3]),
        pltpu.make_async_copy(gm_v, gm, out_sem.at[4]),
    ]
    for c in loads:
        c.start()
    for p in range(2):
        loads[p].wait()
        for q in range(SIDE):
            for b in range(SIDE):
                piece = go_v[0, b, q] if p == 0 else go_v[1, q, b]
                go_f[p, b * rq:(b + 1) * rq, q * fq:(q + 1) * fq] = piece.astype(F32)
        outs[p].start()
    for i in (3, 4):
        loads[i].wait()
        outs[i].start()
    loads[2].wait()
    for p in range(2):
        for b in range(per):
            gi_f[p, b * out_rows:(b + 1) * out_rows, :] = gi_v[p * per + b].astype(F32)
    outs[2].start()
    for c in outs:
        c.wait()


def solution(mesh):
    n_row = mesh.shape["row"]

    def on_device(tokens, weights, adapter_in, adapter_out, magnitude, hidden_cot):
        share, depth = tokens.shape
        rank = adapter_in.shape[1]
        width = adapter_out.shape[2]
        fq = width // SIDE
        tb = share * n_row // SIDE
        rq = rank // SIDE
        own_rows = tb // SIDE
        pr = 2 * rank
        vm = pltpu.VMEM
        dma = pltpu.SemaphoreType.DMA
        scratch = [
            vm((SIDE * tb, depth), BF16),
            vm((2, SIDE, depth, fq), BF16),
            vm((2, SIDE, SIDE, tb, fq), BF16),
            vm((2, rank, depth), BF16),
            vm((SIDE, 2, rank, fq), BF16),
            vm((2, width), F32),
            vm((2, depth, rank), BF16),
            vm((2, SIDE, tb, fq), BF16),
            vm((2, 2, SIDE, tb, fq), BF16),
            vm((2, tb, fq), BF16),
            vm((2, 2, tb, fq), BF16),
            vm((SIDE, own_rows, fq), BF16),
            vm((SIDE, 2, fq), F32),
            vm((2, fq), F32),
            vm((SIDE, 2, fq), F32),
            vm((SIDE, 2, fq), F32),
            vm((SIDE, pr, tb), BF16),
            vm((pr, tb), BF16),
            vm((pr, tb), BF16),
            vm((SIDE, pr, tb), BF16),
            vm((SIDE, pr, tb), BF16),
            vm((SIDE, own_rows, fq), BF16),
            vm((SIDE, own_rows, fq), BF16),
            vm((2, tb, fq), BF16),
            vm((2, fq), F32),
            vm((SIDE, 2, fq), F32),
            vm((4, fq), F32),
            vm((SIDE, 4, fq), F32),
            vm((2, width), F32),
            vm((SIDE, 2, rq, fq), BF16),
            vm((SIDE, 2, rq, fq), BF16),
            vm((pr, tb), BF16),
            vm((pr, tb), BF16),
            vm((SIDE, pr, tb), BF16),
            vm((SIDE, pr, tb), BF16),
            vm((2, SIDE, SIDE, rq, fq), BF16),
            vm((2, SIDE, SIDE, rq, fq), BF16),
            vm((2, SIDE, rq, fq), BF16),
            vm((2, SIDE, rq, fq), BF16),
            vm((2, SIDE, SIDE, rq, fq), BF16),
            vm((n_row, pr // n_row, depth), BF16),
            vm((n_row, pr // n_row, depth), BF16),
            vm((pr // n_row, depth), BF16),
            vm((n_row, pr // n_row, depth), BF16),
            vm((2, rank, depth), F32),
            dma((2 * SIDE,)),
            dma((SIDE,)),
            dma((4,)),
            dma((4,)),
            dma((SIDE,)),
            dma((2 * SIDE * SIDE,)),
            dma((2 * SIDE * SIDE,)),
            dma((n_row,)),
            dma((n_row,)),
            dma((12 * SIDE,)),
            dma((12 * SIDE,)),
            dma((12,)),
            dma((12,)),
            dma((5 * SIDE,)),
            dma((5 * SIDE,)),
            dma((EXCHANGES * 8,)),
            dma((EXCHANGES * 8,)),
        ]
        anywhere = pl.BlockSpec(memory_space=pl.ANY)
        parts = pl.pallas_call(
            functools.partial(kernel, n_row),
            out_shape=(
                jax.ShapeDtypeStruct(hidden_cot.shape, BF16),
                jax.ShapeDtypeStruct((n_row, pr // n_row, depth), BF16),
                jax.ShapeDtypeStruct((2, SIDE, SIDE, rq, fq), BF16),
                jax.ShapeDtypeStruct(magnitude.shape, F32),
            ),
            in_specs=[anywhere] * 6,
            out_specs=(anywhere,) * 4,
            scratch_shapes=scratch,
            compiler_params=pltpu.CompilerParams(
                collective_id=0, has_side_effects=True, vmem_limit_bytes=67_043_328
            ),
        )(tokens, weights, adapter_in, adapter_out, magnitude, hidden_cot)
        return pl.pallas_call(
            finish_kernel,
            out_shape=(
                jax.ShapeDtypeStruct(hidden_cot.shape, BF16),
                jax.ShapeDtypeStruct(adapter_in.shape, F32),
                jax.ShapeDtypeStruct(adapter_out.shape, F32),
                jax.ShapeDtypeStruct(magnitude.shape, F32),
            ),
            in_specs=[anywhere] * 4,
            out_specs=(anywhere,) * 4,
            scratch_shapes=[
                vm(hidden_cot.shape, BF16),
                vm((n_row, pr // n_row, depth), BF16),
                vm((2, SIDE, SIDE, rq, fq), BF16),
                vm(magnitude.shape, F32),
                vm(adapter_in.shape, F32),
                vm(adapter_out.shape, F32),
                dma((5,)),
                dma((5,)),
            ],
            compiler_params=pltpu.CompilerParams(vmem_limit_bytes=67_043_328),
        )(*parts)

    in_specs = (
        P("row", "col"),
        P(None, "col", "row"),
        P(None, None, "col"),
        P(None, None, "row"),
        P(None, "row"),
        P("col", "row"),
    )
    out_specs = (P("col", "row"), P(None, None, "col"), P(None, None, "row"), P(None, "row"))
    return jax.shard_map(
        on_device, mesh=mesh, in_specs=in_specs, out_specs=out_specs, check_vma=False
    )
```

```python
import functools

import jax
import jax.numpy as jnp
from jax import lax
from jax.experimental import pallas as pl
from jax.experimental.pallas import tpu as pltpu
from jax.sharding import PartitionSpec as P

EPSILON = 1e-06
F32 = jnp.float32
BF16 = jnp.bfloat16
MESH = pl.DeviceIdType.MESH
SIDE = 4
ORDER = (2, 1, 3, 0)
EXCHANGES = 19
FAR, RAW, ACC = 0, 1, 2


def nt_dot(a, b):
    return lax.dot_general(a, b, (((1,), (1,)), ((), ())), preferred_element_type=F32)


def kernel(n_row, tok, w_hbm, ain, aout, mag, cot, hid_out, giall, gall, gm_out,
           lhs, wb, pp, ainv, aoutv, magv, ain_t, rfar, rnear, sfar, snear, cotq, ssb, ssx, ssr, ssr2,
           zb, zx, zs, zr, zr2, hidq, hidr, dsc, st, strr, bb, ball, g1, g1r,
           wv, wx, wr, wall, qq, qr, qx, qr2, gib, gir, gio, tin,
           w_sem, a_sem, in_sem, gat_s, gat_r, tok_s, tok_r, main_s, main_r, ph2_s, ph2_r, q_s, q_r, ex_s, ex_r):
    row, col = lax.axis_index("row"), lax.axis_index("col")
    y, x = col // SIDE, col % SIDE
    n_z = n_row // 2
    z, core = row // 2, row % 2
    share, depth = tok.shape
    rank = ain.shape[1]
    width = aout.shape[2]
    fq = width // SIDE
    tb = share * n_row // SIDE
    rq = rank // SIDE
    own_rows = tb // SIDE
    half = tb // 2
    top, bottom = pl.ds(0, half), pl.ds(half, half)
    first, second = (x, y), (y, x)

    def wrap(v):
        return (v + 2 * SIDE) % SIDE

    def at_x(k):
        return (row, y * SIDE + wrap(x + k))

    def at_y(k):
        return (row, wrap(y + k) * SIDE + x)

    def at_row(k):
        return ((row + k) % n_row, col)

    def at_core():
        return (z * 2 + (1 - core), col)

    def at_z(k):
        return (((z + k) % n_z) * 2 + core, col)

    ring1 = (at_x, at_y)
    ring2 = (at_y, at_x)

    def quarter(q):
        return pl.ds(pl.multiple_of(q * fq, 128), fq)

    def offset(m):
        return (2 - m + 3 * ((m * (m - 1)) // 2) + 8) % SIDE

    barrier = pltpu.get_barrier_semaphore()
    peers = [at_x(k) for k in (1, 2, 3)] + [at_y(k) for k in (1, 2, 3)]
    peers += [at_row(k) for k in range(1, n_row)]
    for peer in peers:
        pl.semaphore_signal(barrier, inc=1, device_id=peer, device_id_type=MESH)

    def own_tokens():
        return lhs.at[pl.ds(pl.multiple_of(row * share, 16), share), :]

    loads = [
        pltpu.make_async_copy(ain, ainv, in_sem.at[0]),
        pltpu.make_async_copy(tok, own_tokens(), in_sem.at[1]),
        pltpu.make_async_copy(mag, magv, in_sem.at[2]),
        pltpu.make_async_copy(cot.at[:, quarter(x)], cotq.at[x], in_sem.at[3]),
    ]

    def w_copy(p, q):
        return pltpu.make_async_copy(
            w_hbm.at[p, :, quarter(q)], wb.at[p, q], w_sem.at[p * SIDE + q])

    def out_copy(q):
        return pltpu.make_async_copy(aout.at[:, :, quarter(q)], aoutv.at[q], a_sem.at[q])

    loads[1].start()
    loads[0].start()
    for j in ORDER:
        out_copy(wrap(x + j)).start()
        for p in range(2):
            w_copy(p, wrap(x + j)).start()
        if j == ORDER[0]:
            for c in loads[2:]:
                c.start()

    def remote(src, dst, send, recv, peer):
        return pltpu.make_async_remote_copy(
            src_ref=src, dst_ref=dst, send_sem=send, recv_sem=recv,
            device_id=peer, device_id_type=MESH)

    def tok_rows(owner):
        return lhs.at[pl.ds(pl.multiple_of(owner * share, 16), share), :]

    def tok_copy(i):
        if i == 0:
            owner, peer = row, at_core()
        elif i < n_z:
            owner, peer = row, at_z(i)
        else:
            owner = ((z + n_z - (i - n_z + 1)) % n_z) * 2 + core
            peer = at_core()
        return remote(tok_rows(owner), tok_rows(owner), tok_s.at[i], tok_r.at[i], peer)

    n_tok = 2 * n_z - 1
    z_order = list(range(2, n_z - 1)) + [1, n_z - 1]

    def peers_of(count):
        return (2, 1, 3) if count == SIDE else range(1, count)

    def exchange(e, peer_of, count, src, dst):
        return [remote(src(k), dst(k), ex_s.at[e * 8 + k], ex_r.at[e * 8 + k], peer_of(k))
                for k in peers_of(count)]

    started = []

    def begin(copies):
        for c in copies:
            c.start()
        started.extend(copies)
        return copies

    def arrive(copies):
        for c in copies:
            c.wait_recv()

    def q_first(p, k, j):
        if p == 0:
            src, dst, i = qq.at[0, wrap(x + k)], qr.at[0, k], k
        else:
            q = wrap(x + j)
            src, dst, i = qq.at[1, wrap(y + k), q], qr.at[1, k, q], SIDE + k * SIDE + j
        return remote(src, dst, q_s.at[i], q_r.at[i], ring1[p](k))

    cot_x = exchange(0, at_x, SIDE, lambda k: cot.at[:, quarter(wrap(x + k))], lambda k: cotq.at[x])

    pl.semaphore_wait(barrier, len(peers))
    loads[1].wait()
    for i in z_order + [0]:
        tok_copy(i).start()
    for c in cot_x:
        c.start()

    loads[0].wait()
    for p in range(2):
        ain_t[p] = ainv[p].astype(F32).T.astype(BF16)
    step = min(128, depth)

    def prepare(m):
        q = wrap(x + offset(m))
        out_copy(q).wait()
        for p in range(2):
            w_copy(p, q).wait()
            left = aoutv[q, p]

            def body(i, acc):
                rows = pl.ds(pl.multiple_of(i * step, step), step)
                low = jnp.dot(ain_t[p, rows, :], left, preferred_element_type=F32)
                d = wb[p, q, rows, :].astype(F32) + low
                wb[p, q, rows, :] = d.astype(BF16)
                return acc + jnp.sum((d * d).reshape(step // 8, 8, fq), axis=0)

            acc = lax.fori_loop(0, depth // step, body, jnp.zeros((8, fq), F32))
            ssb[q, p:p + 1, :] = jnp.sum(acc, axis=0, keepdims=True)
            res = jnp.dot(ainv[p], wb[p, q], preferred_element_type=F32).astype(BF16)
            for b in range(SIDE):
                piece = res[b * rq:(b + 1) * rq, :]
                if p == 0:
                    qq[0, q, b] = piece
                else:
                    qq[1, b, q] = piece

    def q_send(m):
        j = offset(m)

        if not (isinstance(m, int) and m == SIDE - 1):
            q_first(0, j, 0).start()

        for k in (2, 1, 3):
            q_first(1, k, j).start()

    def early(m, carry):
        prepare(m)
        q_send(m)

        return carry

    lax.fori_loop(0, 2, early, 0)

    for i in z_order:
        tok_copy(i).wait_recv()
        tok_copy(n_z - 1 + i).start()
    tok_copy(0).wait_recv()
    for i in range(n_z, n_tok):
        tok_copy(i).wait_recv()

    def product(p, q):
        res = jnp.dot(lhs[...], wb[p, q], preferred_element_type=F32).astype(BF16)
        for b in range(SIDE):
            piece = res[b * tb:(b + 1) * tb, :]
            if p == 0:
                pp[0, q, b] = piece
            else:
                pp[1, b, q] = piece

    def main_copy(p, d, kind, j):
        c1, s = first[p], wrap(second[p] + j)
        peer = ring1[p](1 if d == 0 else -1)
        if kind == FAR:
            rows = top if d == 0 else bottom
            src = pp.at[p, wrap(c1 + 2), s, rows, :]
            dst = rfar.at[p, j, rows, :]
        else:
            rows = top if (d == 0) == (kind == ACC) else bottom
            src = pp.at[p, wrap(c1 + (1 if d == 0 else -1)), s, rows, :]
            dst = rnear.at[p, d, j, rows, :]
        i = ((p * 2 + d) * 3 + kind) * SIDE + j
        return remote(src, dst, main_s.at[i], main_r.at[i], peer)

    def ph2_copy(p, d, kind):
        c1, c2 = first[p], second[p]
        peer = ring2[p](1 if d == 0 else -1)
        if kind == FAR:
            rows = top if d == 0 else bottom
            src = pp.at[p, c1, wrap(c2 + 2), rows, :]
            dst = sfar.at[p, rows, :]
        else:
            rows = top if (d == 0) == (kind == ACC) else bottom
            src = pp.at[p, c1, wrap(c2 + (1 if d == 0 else -1)), rows, :]
            dst = snear.at[p, d, rows, :]
        i = (p * 2 + d) * 3 + kind
        return remote(src, dst, ph2_s.at[i], ph2_r.at[i], peer)

    ss_x = exchange(1, at_x, SIDE, lambda k: ssb.at[wrap(x + k)], lambda k: ssr.at[k])
    z_y = exchange(3, at_y, SIDE, lambda k: zb.at[wrap(y + k)], lambda k: zr.at[k])

    def add_into(dst, src):
        dst[...] = (dst[...].astype(F32) + src[...].astype(F32)).astype(BF16)

    def accumulate(j):
        for p in range(2):
            for d in range(2):
                main_copy(p, d, FAR, j).wait_recv()
                rows = top if d == 0 else bottom
                near = wrap(first[p] + (1 if d == 0 else -1))
                add_into(pp.at[p, near, wrap(second[p] + j), rows, :], rfar.at[p, j, rows, :])

    def send_sums(j):
        for p in range(2):
            for d in range(2):
                main_copy(p, d, ACC, j).start()

    def finish(p, j):
        for d in range(2):
            main_copy(p, d, RAW, j).wait_recv()
            main_copy(p, d, ACC, j).wait_recv()
        mine = pp.at[p, first[p], wrap(second[p] + j)]
        mine[...] = (mine[...].astype(F32) + rnear[p, 0, j].astype(F32)
                     + rnear[p, 1, j].astype(F32)).astype(BF16)

    def second_sum(p, d):
        ph2_copy(p, d, FAR).wait_recv()
        rows = top if d == 0 else bottom
        near = wrap(second[p] + (1 if d == 0 else -1))
        add_into(pp.at[p, first[p], near, rows, :], sfar.at[p, rows, :])
        ph2_copy(p, d, ACC).start()

    def stage(i_p, carry):
        j_p = offset(i_p)
        q = wrap(x + j_p)
        product(1, q)
        for d in range(2):
            main_copy(1, d, FAR, j_p).start()

        @pl.when(i_p < 3)
        def _():
            for d in range(2):
                main_copy(1, d, RAW, j_p).start()

        product(0, q)

        @pl.when(i_p == 0)
        def _():
            for j in ORDER:
                for d in range(2):
                    main_copy(0, d, FAR, j).start()

        @pl.when(i_p == 1)
        def _():
            for j in ORDER[:3]:
                main_copy(0, 0, RAW, j).start()

        @pl.when(i_p == 2)
        def _():
            for j in ORDER[:3]:
                main_copy(0, 1, RAW, j).start()

        @pl.when(i_p < 2)
        def _():
            prepare(i_p + 2)

            @pl.when(i_p == 1)
            def _():
                for c in ss_x:
                    c.start()

        @pl.when(i_p == 2)
        def _():
            accumulate(2)
            send_sums(2)

        @pl.when(i_p == 3)
        def _():
            accumulate(1)
            send_sums(1)

        return carry

    lax.fori_loop(0, SIDE, stage, 0)

    accumulate(3)
    send_sums(3)
    ain_all = ainv[...].reshape(2 * rank, depth)
    for b in range(SIDE):
        zb[b] = nt_dot(ain_all, lhs[b * tb:(b + 1) * tb, :]).astype(BF16)
    for c in z_y:
        c.start()
    accumulate(0)

    for p in range(2):
        finish(p, 2)
        for d in range(2):
            ph2_copy(p, d, FAR).start()
    for p in range(2):
        for d in range(2):
            main_copy(p, d, RAW, 0).start()
    for p in range(2):
        finish(p, 1)
        ph2_copy(p, 0, RAW).start()
    arrive(ss_x)
    ssx[...] = ssb[x] + ssr[1] + ssr[2] + ssr[3]
    ss_y = begin(exchange(2, at_y, SIDE, lambda k: ssx, lambda k: ssr2.at[k]))
    for p in range(2):
        second_sum(p, 0)
    for p in range(2):
        finish(p, 3)
        ph2_copy(p, 1, RAW).start()
    for p in range(2):
        second_sum(p, 1)
    for p in range(2):
        for d in range(2):
            main_copy(p, d, ACC, 0).start()
    arrive(z_y)
    zx[...] = (zb[y].astype(F32) + zr[1].astype(F32) + zr[2].astype(F32)
               + zr[3].astype(F32)).astype(BF16)
    z_x = begin(exchange(4, at_x, SIDE, lambda k: zx, lambda k: zr2.at[k]))
    q_send(2)
    q_send(3)
    arrive(ss_y)
    total = ssx[...] + ssr2[1] + ssr2[2] + ssr2[3]
    norm = jnp.sqrt(total + EPSILON)
    loads[2].wait()
    mag_q = magv[:, quarter(x)]
    coef = mag_q / norm
    arrive(cot_x)
    loads[3].wait()

    for p in range(2):
        finish(p, 0)
    for p in range(2):
        for d in range(2):
            ph2_copy(p, d, RAW).wait_recv()
            ph2_copy(p, d, ACC).wait_recv()

    def summed(p, rows):
        return (pp[p, first[p], second[p], rows, :].astype(F32)
                + snear[p, 0, rows, :].astype(F32) + snear[p, 1, rows, :].astype(F32))

    coef0, coef1 = coef[0:1], coef[1:2]
    chunk = min(16, own_rows)
    per = own_rows // chunk

    def gating(i, carry):
        acc0, acc1 = carry
        rows = pl.ds(pl.multiple_of(i * chunk, chunk), chunk)
        inner = pl.ds(pl.multiple_of((i % per) * chunk, chunk), chunk)
        raw0, raw1 = summed(0, rows), summed(1, rows)
        gate, up = raw0 * coef0, raw1 * coef1
        sig = jax.nn.sigmoid(gate)
        hidq[i // per, inner, :] = (gate * sig * up).astype(BF16)
        c = cotq[i // per, inner, :].astype(F32)
        d0 = (c * up * sig * (1.0 + gate * (1.0 - sig))).astype(BF16)
        d1 = (c * gate * sig).astype(BF16)
        dsc[0, rows, :] = d0
        dsc[1, rows, :] = d1
        s0 = jnp.sum((d0.astype(F32) * raw0).reshape(chunk // 8, 8, fq), axis=0)
        s1 = jnp.sum((d1.astype(F32) * raw1).reshape(chunk // 8, 8, fq), axis=0)
        return (acc0 + s0, acc1 + s1)

    zero = jnp.zeros((8, fq), F32)
    acc0, acc1 = lax.fori_loop(0, tb // chunk, gating, (zero, zero))
    st[0:1] = jnp.sum(acc0, axis=0, keepdims=True)
    st[1:2] = jnp.sum(acc1, axis=0, keepdims=True)
    st_y = begin(exchange(6, at_y, SIDE, lambda k: st, lambda k: strr.at[k]))

    for p in range(2):
        scaled = (aoutv[x, p].astype(F32) * coef[p:p + 1]).astype(BF16)
        wv[p * rank:(p + 1) * rank, :] = nt_dot(scaled, dsc[p]).astype(BF16)
    w_x = begin(exchange(9, at_x, SIDE, lambda k: wv, lambda k: wr.at[k]))
    arrive(z_x)
    zs[...] = (zx[...].astype(F32) + zr2[1].astype(F32) + zr2[2].astype(F32)
               + zr2[3].astype(F32)).astype(BF16)
    for p in range(2):
        res = jnp.dot(zs[p * rank:(p + 1) * rank, :], dsc[p], preferred_element_type=F32)
        for b in range(SIDE):
            g1[b, p] = res[b * rq:(b + 1) * rq, :].astype(BF16)
    g1_y = begin(exchange(8, at_y, SIDE, lambda k: g1.at[wrap(y + k)], lambda k: g1r.at[k]))
    hidr[x] = hidq[x]

    for k in (2, 1, 3):
        q_first(0, k, 0).wait_recv()
    for j in ORDER:
        for k in (2, 1, 3):
            q_first(1, k, j).wait_recv()
    for p in range(2):
        qx[p] = (qq[p, first[p]].astype(F32) + qr[p, 1].astype(F32) + qr[p, 2].astype(F32)
                 + qr[p, 3].astype(F32)).astype(BF16)
    q_two = [
        begin(exchange(17 + p, ring2[p], SIDE, lambda k, p=p: qx.at[p, wrap(second[p] + k)],
                       lambda k, p=p: qr2.at[p, k]))
        for p in range(2)
    ]
    arrive(st_y)
    stat = st[...] + strr[1] + strr[2] + strr[3]
    tilt = mag_q * stat / (norm * norm * norm)
    bb[0:2] = tilt
    bb[2:4] = stat / norm
    b_x = begin(exchange(7, at_x, SIDE, lambda k: bb, lambda k: ball.at[x]))
    hid_x = begin(exchange(5, at_x, SIDE, lambda k: hidq.at[wrap(x + k)], lambda k: hidr.at[x]))
    ball[x] = bb[...]

    arrive(w_x)
    wx[...] = (wv[...].astype(F32) + wr[1].astype(F32) + wr[2].astype(F32)
               + wr[3].astype(F32)).astype(BF16)
    w_y = begin(exchange(10, at_y, SIDE, lambda k: wx, lambda k: wall.at[y]))
    wall[y] = wx[...]

    def tilted(p, q, b):
        scaled = (aoutv[q, p].astype(F32) * b).astype(BF16)
        return nt_dot(scaled, wb[p, q])

    for p in range(2):
        tin[p] = -tilted(p, x, tilt[p:p + 1])

    arrive(g1_y)
    for p in range(2):
        arrive(q_two[p])
        both = (g1[y, p].astype(F32) + g1r[1, p].astype(F32) + g1r[2, p].astype(F32)
                + g1r[3, p].astype(F32))
        low = (qx[p, second[p]].astype(F32) + qr2[p, 1].astype(F32) + qr2[p, 2].astype(F32)
               + qr2[p, 3].astype(F32))
        gall[p, second[p], first[p]] = (coef[p:p + 1] * both - tilt[p:p + 1] * low).astype(BF16)

    def gat_one(p, k):
        piece = gall.at[p, second[p], first[p]]
        return remote(piece, piece, ex_s.at[(11 + p) * 8 + k], ex_r.at[(11 + p) * 8 + k],
                      ring1[p](k))

    def gat_two(p, i, k):
        piece = gall.at[p, second[p], wrap(first[p] - i)]
        n = (p * SIDE + i) * SIDE + k
        return remote(piece, piece, gat_s.at[n], gat_r.at[n], ring2[p](k))

    for k in (2, 1, 3):
        for p in range(2):
            gat_one(p, k).start()
    for k in (2, 1, 3):
        for p in range(2):
            gat_two(p, 0, k).start()

    arrive(b_x)
    out_rows = 2 * rank // n_row
    for p in range(2):
        t1 = tin[p]
        for k in range(1, SIDE):
            q = wrap(x + k)
            t1 = t1 - tilted(p, q, ball[q, p:p + 1])
        tin[p] = t1
    arrive(w_y)
    for p in range(2):
        t1 = tin[p]
        for b in range(SIDE):
            t1 = t1 + jnp.dot(wall[b, p * rank:(p + 1) * rank, :], lhs[b * tb:(b + 1) * tb, :],
                              preferred_element_type=F32)

        for b in range(rank // out_rows):
            gib[p * (rank // out_rows) + b] = t1[b * out_rows:(b + 1) * out_rows].astype(BF16)
    gi_rs = begin(exchange(15, at_row, n_row, lambda k: gib.at[(row + k) % n_row],
                           lambda k: gir.at[k]))

    for i in (1, 3, 2):
        for p in range(2):
            gat_one(p, i).wait_recv()
            for k in (2, 1, 3):
                gat_two(p, i, k).start()
    for q in range(SIDE):
        gm_out[:, q * fq:(q + 1) * fq] = ball[q, 2:4, :]
    arrive(gi_rs)
    acc = gib[row].astype(F32)
    for k in range(1, n_row):
        acc = acc + gir[k].astype(F32)
    gio[...] = acc.astype(BF16)
    gi_ag = begin(exchange(16, at_row, n_row, lambda k: gio, lambda k: giall.at[row]))
    giall[row] = gio[...]
    arrive(hid_x)
    for q in range(SIDE):
        hid_out[:, q * fq:(q + 1) * fq] = hidr[q]

    for p in range(2):
        for i in range(SIDE):
            for k in (1, 2, 3):
                gat_two(p, i, k).wait_recv()
    arrive(gi_ag)

    for i in range(n_tok):
        tok_copy(i).wait_send()
    for c in cot_x + ss_x + z_y:
        c.wait_send()
    for p in range(2):
        for k in (1, 2, 3):
            gat_one(p, k).wait_send()
            for i in range(SIDE):
                gat_two(p, i, k).wait_send()
    for k in (1, 2, 3):
        q_first(0, k, 0).wait_send()
        for j in range(SIDE):
            q_first(1, k, j).wait_send()
    for p in range(2):
        for d in range(2):
            for kind in range(3):
                for j in range(SIDE):
                    main_copy(p, d, kind, j).wait_send()
                ph2_copy(p, d, kind).wait_send()
    for c in started:
        c.wait_send()


def finish_kernel(hid_in, gi_in, go_in, gm_in, hid, gi, go, gm, gi_f, go_f, out_sem):
    n_row, out_rows = gi_in.shape[:2]
    rq, fq = go_in.shape[3:]
    per = n_row // 2
    outs = [
        pltpu.make_async_copy(go_f.at[0], go.at[0], out_sem.at[0]),
        pltpu.make_async_copy(go_f.at[1], go.at[1], out_sem.at[1]),
        pltpu.make_async_copy(gi_f, gi, out_sem.at[2]),
        pltpu.make_async_copy(hid_in, hid, out_sem.at[3]),
        pltpu.make_async_copy(gm_in, gm, out_sem.at[4]),
    ]
    for p in range(2):
        for q in range(SIDE):
            for b in range(SIDE):
                piece = go_in[0, b, q] if p == 0 else go_in[1, q, b]
                go_f[p, b * rq:(b + 1) * rq, q * fq:(q + 1) * fq] = piece.astype(F32)
        outs[p].start()
    outs[3].start()
    outs[4].start()
    for p in range(2):
        for b in range(per):
            gi_f[p, b * out_rows:(b + 1) * out_rows, :] = gi_in[p * per + b].astype(F32)
    outs[2].start()
    for c in outs:
        c.wait()


def solution(mesh):
    n_row = mesh.shape["row"]

    def on_device(tokens, weights, adapter_in, adapter_out, magnitude, hidden_cot):
        share, depth = tokens.shape
        rank = adapter_in.shape[1]
        width = adapter_out.shape[2]
        fq = width // SIDE
        tb = share * n_row // SIDE
        rq = rank // SIDE
        own_rows = tb // SIDE
        pr = 2 * rank
        vm = pltpu.VMEM
        dma = pltpu.SemaphoreType.DMA
        scratch = [
            vm((SIDE * tb, depth), BF16),
            vm((2, SIDE, depth, fq), BF16),
            vm((2, SIDE, SIDE, tb, fq), BF16),
            vm((2, rank, depth), BF16),
            vm((SIDE, 2, rank, fq), BF16),
            vm((2, width), F32),
            vm((2, depth, rank), BF16),
            vm((2, SIDE, tb, fq), BF16),
            vm((2, 2, SIDE, tb, fq), BF16),
            vm((2, tb, fq), BF16),
            vm((2, 2, tb, fq), BF16),
            vm((SIDE, own_rows, fq), BF16),
            vm((SIDE, 2, fq), F32),
            vm((2, fq), F32),
            vm((SIDE, 2, fq), F32),
            vm((SIDE, 2, fq), F32),
            vm((SIDE, pr, tb), BF16),
            vm((pr, tb), BF16),
            vm((pr, tb), BF16),
            vm((SIDE, pr, tb), BF16),
            vm((SIDE, pr, tb), BF16),
            vm((SIDE, own_rows, fq), BF16),
            vm((SIDE, own_rows, fq), BF16),
            vm((2, tb, fq), BF16),
            vm((2, fq), F32),
            vm((SIDE, 2, fq), F32),
            vm((4, fq), F32),
            vm((SIDE, 4, fq), F32),
            vm((SIDE, 2, rq, fq), BF16),
            vm((SIDE, 2, rq, fq), BF16),
            vm((pr, tb), BF16),
            vm((pr, tb), BF16),
            vm((SIDE, pr, tb), BF16),
            vm((SIDE, pr, tb), BF16),
            vm((2, SIDE, SIDE, rq, fq), BF16),
            vm((2, SIDE, SIDE, rq, fq), BF16),
            vm((2, SIDE, rq, fq), BF16),
            vm((2, SIDE, rq, fq), BF16),
            vm((n_row, pr // n_row, depth), BF16),
            vm((n_row, pr // n_row, depth), BF16),
            vm((pr // n_row, depth), BF16),
            vm((2, rank, depth), F32),
            dma((2 * SIDE,)),
            dma((SIDE,)),
            dma((4,)),
            dma((2 * SIDE * SIDE,)),
            dma((2 * SIDE * SIDE,)),
            dma((n_row,)),
            dma((n_row,)),
            dma((12 * SIDE,)),
            dma((12 * SIDE,)),
            dma((12,)),
            dma((12,)),
            dma((5 * SIDE,)),
            dma((5 * SIDE,)),
            dma((EXCHANGES * 8,)),
            dma((EXCHANGES * 8,)),
        ]
        anywhere = pl.BlockSpec(memory_space=pl.ANY)
        arrays = (tokens, weights, adapter_in, adapter_out, magnitude, hidden_cot)
        parts = pl.pallas_call(
            functools.partial(kernel, n_row),
            out_shape=(
                jax.ShapeDtypeStruct(hidden_cot.shape, BF16),
                jax.ShapeDtypeStruct((n_row, pr // n_row, depth), BF16),
                jax.ShapeDtypeStruct((2, SIDE, SIDE, rq, fq), BF16),
                jax.ShapeDtypeStruct(magnitude.shape, F32),
            ),
            in_specs=[pl.BlockSpec(memory_space=pltpu.HBM)] * 6,
            out_specs=(pl.BlockSpec(memory_space=pltpu.VMEM),) * 4,
            scratch_shapes=scratch,
            compiler_params=pltpu.CompilerParams(
                collective_id=0, has_side_effects=True, vmem_limit_bytes=44 * 2**20
            ),
        )(*[pltpu.with_memory_space_constraint(a, pltpu.HBM) for a in arrays])
        return pl.pallas_call(
            finish_kernel,
            out_shape=(
                jax.ShapeDtypeStruct(hidden_cot.shape, BF16),
                jax.ShapeDtypeStruct(adapter_in.shape, F32),
                jax.ShapeDtypeStruct(adapter_out.shape, F32),
                jax.ShapeDtypeStruct(magnitude.shape, F32),
            ),
            in_specs=[pl.BlockSpec(memory_space=pltpu.VMEM)] * 4,
            out_specs=(anywhere,) * 4,
            scratch_shapes=[
                vm(adapter_in.shape, F32),
                vm(adapter_out.shape, F32),
                dma((5,)),
            ],
            compiler_params=pltpu.CompilerParams(vmem_limit_bytes=8 * 2**20),
        )(*parts)

    in_specs = (
        P("row", "col"),
        P(None, "col", "row"),
        P(None, None, "col"),
        P(None, None, "row"),
        P(None, "row"),
        P("col", "row"),
    )
    out_specs = (P("col", "row"), P(None, None, "col"), P(None, None, "row"), P(None, "row"))
    return jax.shard_map(
        on_device, mesh=mesh, in_specs=in_specs, out_specs=out_specs, check_vma=False
    )
```
